32 devices in a mesh: slab: 8 (over z, x), depth: 4 (over y, core).
Axes of the slice: x: 2, y: 2, z: 4, core: 2. Of those that a mesh axis runs over, the one named last changes fastest.
Arguments:
- generating_displacement: float32 [3, 32, 16, 512], P(None, 'slab', 'depth'), may hold values from -0.6 to 0.6
- generating_velocity: float32 [3, 32, 16, 512], P(None, 'slab', 'depth'), may hold values from -6 to 6
- generating_memory: float32 [3, 5, 5, 5, 5, 8, 4, 128], P(None, None, None, None, None, 'slab', 'depth'), may hold values from -1.8 to 1.8
- correlation_displacement: float32 [3, 32, 16, 512], P(None, 'slab', 'depth'), may hold values from -0.6 to 0.6
- correlation_velocity: float32 [3, 32, 16, 512], P(None, 'slab', 'depth'), may hold values from -6 to 6
- correlation_memory: float32 [3, 5, 5, 5, 5, 8, 4, 128], P(None, None, None, None, None, 'slab', 'depth'), may hold values from -1.8 to 1.8
- first_lame: float32 [5, 5, 5, 8, 4, 128], P(None, None, None, 'slab', 'depth'), may hold values from 0.5 to 1.5
- shear_modulus: float32 [5, 5, 5, 8, 4, 128], P(None, None, None, 'slab', 'depth'), may hold values from 0.5 to 1
- modulus_defect: float32 [5, 5, 5, 8, 4, 128], P(None, None, None, 'slab', 'depth'), may hold values from 0.05 to 0.3
- relaxation_keep: float32 [3], replicated, may hold values from 0.5 to 0.98
- density: float32 [32, 16, 512], P('slab', 'depth'), may hold values from 0.8 to 1.6
- surface_history: float32 [64, 32, 512], P(None, 'slab', 'depth'), may hold values from -0.6 to 0.6
- node_cell: int32 [32, 512], P('slab', 'depth'), may hold values from 0 to 255
- cell_filters: float32 [256, 64], replicated, may hold values from -0.75 to 0.75
Outputs:
- generating_displacement_next: float32 [3, 32, 16, 512], P(None, 'slab', 'depth')
- generating_velocity_next: float32 [3, 32, 16, 512], P(None, 'slab', 'depth')
- generating_memory_next: float32 [3, 5, 5, 5, 5, 8, 4, 128], P(None, None, None, None, None, 'slab', 'depth')
- correlation_displacement_next: float32 [3, 32, 16, 512], P(None, 'slab', 'depth')
- correlation_velocity_next: float32 [3, 32, 16, 512], P(None, 'slab', 'depth')
- correlation_memory_next: float32 [3, 5, 5, 5, 5, 8, 4, 128], P(None, None, None, None, None, 'slab', 'depth')
The draws below stay inside these ranges and needn't reach their ends.
Inputs may be any that keep to these rules, and one draw needn't show every extreme that they name: node_cell gives each surface node's source cell.
All inputs are finite; a program needn't handle non-finite values.
Results may differ from the reference program's by a relative error of at most 0.0001.
Values sent between devices are 32-bit elements; how exact they have to be, the bound alone decides.
No kernel may reach another device: no remote copies, remote signals or barrier semaphores. Data moves between devices by JAX's collectives and lax.ppermute only.
A program may use at most 128 MiB of HBM per device.

```python
import math
import jax
import jax.numpy as jnp
import numpy as np
from jax import lax

GLL = 5
N_SLS = 3
STEPS = 4
TAPS = 64
CELLS = 256
EZ = 128
NEX = 8
NEY = 4
NX = 32
NY = 16
NZ = 512


def touch_ends(result, rng, least, high):
    place = [jax.random.randint(jax.random.fold_in(rng, axis), (), 0, length) for axis, length in enumerate(result.shape)]
    longest = result.shape.index(max(result.shape))
    beside = place[:longest] + [(place[longest] + 1) % result.shape[longest]] + place[longest + 1:]
    return result.at[tuple(place)].set(least).at[tuple(beside)].set(high)


def shard_levels(rng, extent, shards, least, largest):
    factor_of, own = 1.0, jax.random.fold_in(rng, 6)
    for dim, shards_of in shards:
        steps = jnp.exp(jax.random.uniform(jax.random.fold_in(own, dim), (shards_of,), jnp.float32, least / len(shards), largest / len(shards)))
        factor_of = factor_of * jnp.repeat(steps, extent[dim] // shards_of).reshape([-1 if axis == dim else 1 for axis in range(len(extent))])
    return factor_of


def scatter_about(stream_key, dims, deviation, reach, split=(), held_as=jnp.bfloat16):
    gain = shard_levels(stream_key, dims, split, -0.22, 0.18) if split else 1.0
    values = jax.random.normal(stream_key, dims, jnp.float32) * deviation * gain
    return jnp.minimum(jnp.maximum(values, -reach), reach).astype(held_as)


def setup_inputs(seed: int = 0) -> dict:
    keys = jax.random.split(jax.random.key(seed), 15)
    return {
        "generating_displacement": scatter_about(keys[0], (3, NX, NY, NZ), 0.1, 0.6, ((1, 8), (2, 4)), jnp.float32),
        "generating_velocity": scatter_about(keys[1], (3, NX, NY, NZ), 1.0, 6.0, ((1, 8), (2, 4)), jnp.float32),
        "generating_memory": scatter_about(keys[2], (N_SLS, 5, GLL, GLL, GLL, NEX, NEY, EZ), 0.3, 1.8, ((5, 8), (6, 4)), jnp.float32),
        "correlation_displacement": scatter_about(keys[3], (3, NX, NY, NZ), 0.1, 0.6, ((1, 8), (2, 4)), jnp.float32),
        "correlation_velocity": scatter_about(keys[4], (3, NX, NY, NZ), 1.0, 6.0, ((1, 8), (2, 4)), jnp.float32),
        "correlation_memory": scatter_about(keys[5], (N_SLS, 5, GLL, GLL, GLL, NEX, NEY, EZ), 0.3, 1.8, ((5, 8), (6, 4)), jnp.float32),
        "first_lame": jnp.clip(0.5 + 1.0 * jax.random.uniform(keys[6], (GLL, GLL, GLL, NEX, NEY, EZ), jnp.float32) ** shard_levels(keys[6], (GLL, GLL, GLL, NEX, NEY, EZ), ((3, 8), (4, 4)), -0.2, 0.2), 0.5, 1.5),
        "shear_modulus": jnp.clip(0.5 + 0.5 * jax.random.uniform(keys[7], (GLL, GLL, GLL, NEX, NEY, EZ), jnp.float32) ** shard_levels(keys[7], (GLL, GLL, GLL, NEX, NEY, EZ), ((3, 8), (4, 4)), -0.2, 0.2), 0.5, 1.0),
        "modulus_defect": jnp.clip(jnp.exp(math.log(0.3) - 1.7917595 * jax.random.uniform(keys[8], (GLL, GLL, GLL, NEX, NEY, EZ), jnp.float32) ** shard_levels(keys[8], (GLL, GLL, GLL, NEX, NEY, EZ), ((3, 8), (4, 4)), -0.2, 0.2)), 0.05, 0.3),
        "relaxation_keep": jnp.clip(jax.random.uniform(keys[9], (N_SLS,), jnp.float32, 0.5, 0.98), 0.5, 0.98),
        "density": jnp.clip(0.8 + 0.8 * jax.random.uniform(keys[10], (NX, NY, NZ), jnp.float32) ** shard_levels(keys[10], (NX, NY, NZ), ((0, 8), (1, 4)), -0.2, 0.2), 0.8, 1.6),
        "surface_history": scatter_about(keys[11], (TAPS, NX, NZ), 0.1, 0.6, ((1, 8), (2, 4)), jnp.float32),
        "node_cell": touch_ends(jax.random.randint(keys[12], (NX, NZ), 0, CELLS), jax.random.fold_in(keys[12], 1), 0, CELLS - 1).astype(jnp.int32),
        "cell_filters": scatter_about(keys[13], (CELLS, TAPS), TAPS ** -0.5, 0.75, (), jnp.float32),
    }


time_step = 0.04
highest = lax.Precision.HIGHEST

def gll_tables():
    points = np.array([-1.0, -np.sqrt(3.0 / 7.0), 0.0, np.sqrt(3.0 / 7.0), 1.0])
    weights = np.array([0.1, 49.0 / 90.0, 32.0 / 45.0, 49.0 / 90.0, 0.1])
    number = points.shape[0]
    products = np.array([np.prod([points[target] - points[others] for others in range(number) if others != target]) for target in range(number)])
    derivative = np.zeros((number, number))
    for target in range(number):
        for source in range(number):
            if target == source:
                derivative[target, source] = np.sum([1.0 / (points[target] - points[others]) for others in range(number) if others != target])
            else:
                derivative[target, source] = products[target] / products[source] / (points[target] - points[source])
    return (derivative, weights)

def weight_table(weights_np):
    return weights_np[:, None, None] * weights_np[None, :, None] * weights_np[None, None, :]

def expand_axis(array, position, elements):
    return jnp.stack([lax.slice_in_dim(array, offset, offset + 4 * (elements - 1) + 1, stride=4, axis=position) for offset in range(5)], axis=0)

def to_local(extended):
    count_x = (extended.shape[1] - 1) // 4
    count_y = (extended.shape[2] - 1) // 4
    count_z = (extended.shape[3] - 1) // 4
    section = expand_axis(extended, 1, count_x)
    section = expand_axis(section, 3, count_y)
    section = expand_axis(section, 5, count_z)
    return jnp.transpose(section, (3, 2, 1, 0, 4, 5, 6))

def fold_axis(local, local_axis, element_axis):
    moved = jnp.moveaxis(local, (local_axis, element_axis), (0, -1))
    rest_shape = moved.shape[1:-1]
    elements = moved.shape[-1]
    blank = jnp.zeros_like(moved[0])
    leading = jnp.stack([moved[0], moved[1], moved[2], moved[3]], axis=-1).reshape(rest_shape + (4 * elements,))
    trailing = jnp.stack([moved[4], blank, blank, blank], axis=-1).reshape(rest_shape + (4 * elements,))
    pad_one = jnp.zeros(rest_shape + (1,), jnp.float32)
    pad_four = jnp.zeros(rest_shape + (4,), jnp.float32)
    return jnp.concatenate([leading, pad_one], axis=-1) + jnp.concatenate([pad_four, trailing[..., :4 * elements - 3]], axis=-1)

def from_local(local_force):
    section = fold_axis(local_force, 3, 6)
    section = fold_axis(section, 2, 4)
    section = fold_axis(section, 1, 2)
    return jnp.transpose(section, (0, 3, 2, 1))

def element_force(local_disp, memory, first_lame, shear_modulus, modulus_defect, relaxation_keep, derivative, weight_cube):
    grad_x = jnp.einsum('pq,iqbcxyz->ipbcxyz', derivative, local_disp, precision=highest)
    grad_y = jnp.einsum('pq,iaqcxyz->iapcxyz', derivative, local_disp, precision=highest)
    grad_z = jnp.einsum('pq,iabqxyz->iabpxyz', derivative, local_disp, precision=highest)
    strain_xx = grad_x[0]
    strain_yy = grad_y[1]
    strain_zz = grad_z[2]
    strain_xy = 0.5 * (grad_y[0] + grad_x[1])
    strain_xz = 0.5 * (grad_z[0] + grad_x[2])
    strain_yz = 0.5 * (grad_z[1] + grad_y[2])
    volume_strain = strain_xx + strain_yy + strain_zz
    deviator = jnp.stack([strain_xx - volume_strain / 3.0, strain_yy - volume_strain / 3.0, strain_xy, strain_xz, strain_yz])
    relaxed = lax.optimization_barrier(jnp.sum(memory, axis=0))
    double_shear = 2.0 * shear_modulus
    pressure = first_lame * volume_strain
    stress_xx = pressure + double_shear * strain_xx - relaxed[0]
    stress_yy = pressure + double_shear * strain_yy - relaxed[1]
    stress_zz = pressure + double_shear * strain_zz + relaxed[0] + relaxed[1]
    stress_xy = double_shear * strain_xy - relaxed[2]
    stress_xz = double_shear * strain_xz - relaxed[3]
    stress_yz = double_shear * strain_yz - relaxed[4]
    flux_x = weight_cube * jnp.stack([stress_xx, stress_xy, stress_xz])
    flux_y = weight_cube * jnp.stack([stress_xy, stress_yy, stress_yz])
    flux_z = weight_cube * jnp.stack([stress_xz, stress_yz, stress_zz])
    local_force = jnp.einsum('pq,ipbcxyz->iqbcxyz', derivative, flux_x, precision=highest)
    local_force = local_force + jnp.einsum('pq,iapcxyz->iaqcxyz', derivative, flux_y, precision=highest)
    local_force = local_force + jnp.einsum('pq,iabpxyz->iabqxyz', derivative, flux_z, precision=highest)
    retention = relaxation_keep.reshape((-1, 1, 1, 1, 1, 1, 1, 1))
    memory_next = retention * memory + (1.0 - retention) * (modulus_defect * double_shear * deviator)[None]
    return (local_force, memory_next)

def node_weights(length, first_index, free_top):
    global_index = first_index + jnp.arange(length, dtype=jnp.int32)
    residue = global_index % 4
    values = jnp.where(residue == 0, 0.2, jnp.where(residue == 2, 32.0 / 45.0, 49.0 / 90.0))
    if free_top:
        values = jnp.where(global_index == 0, 0.1, values)
    return values.astype(jnp.float32)

def stiffness(displacement, memory, material):
    nodes_x, nodes_y, nodes_z = displacement.shape[1:]
    extended = jnp.concatenate([displacement, displacement[:, :1]], axis=1)
    extended = jnp.concatenate([extended, jnp.zeros_like(extended[:, :, :1])], axis=2)
    extended = jnp.concatenate([extended, extended[:, :, :, :1]], axis=3)
    local_force, memory_next = element_force(to_local(extended), memory, *material)
    assembled = from_local(local_force)
    assembled = assembled[:, :, :nodes_y]
    assembled = assembled[:, :nodes_x].at[:, 0].add(assembled[:, nodes_x])
    assembled = assembled[..., :nodes_z].at[..., 0].add(assembled[..., nodes_z])
    return (assembled, memory_next)

def reference(generating_displacement, generating_velocity, generating_memory, correlation_displacement, correlation_velocity, correlation_memory, first_lame, shear_modulus, modulus_defect, relaxation_keep, density, surface_history, node_cell, cell_filters):
    derivative_np, weights_np = gll_tables()
    derivative = jnp.asarray(derivative_np, jnp.float32)
    weight_cube = jnp.asarray(weight_table(weights_np)[:, :, :, None, None, None], jnp.float32)
    material = (first_lame, shear_modulus, modulus_defect, relaxation_keep, derivative, weight_cube)
    nodes_x, nodes_y, nodes_z = density.shape
    nodal_mass = density * node_weights(nodes_x, 0, False)[:, None, None] * node_weights(nodes_y, 0, True)[None, :, None] * node_weights(nodes_z, 0, False)[None, None, :]

    def advance(displacement, velocity, memory, surface_force):
        internal, memory = stiffness(displacement, memory, material)
        external = jnp.zeros_like(displacement).at[1, :, 0, :].set(surface_force)
        velocity = velocity + time_step * (external - internal) / nodal_mass
        displacement = displacement + time_step * velocity
        return (displacement, velocity, memory)
    displacement, velocity, memory = (generating_displacement, generating_velocity, generating_memory)
    silent = jnp.zeros((nodes_x, nodes_z), jnp.float32)
    samples = []
    for step_index in range(STEPS):
        displacement, velocity, memory = advance(displacement, velocity, memory, silent)
        samples.append(displacement[1, :, 0, :])
    generated = (displacement, velocity, memory)
    window = jnp.concatenate([surface_history, jnp.stack(samples)], axis=0)
    taps = jnp.moveaxis(jnp.take(cell_filters, node_cell, axis=0), 2, 0)
    forcing = [lax.optimization_barrier(jnp.sum(taps * window[lag + 1:lag + 1 + TAPS], axis=0)) for lag in range(STEPS)]
    displacement, velocity, memory = (correlation_displacement, correlation_velocity, correlation_memory)
    for step_index in range(STEPS):
        displacement, velocity, memory = advance(displacement, velocity, memory, forcing[step_index])
    return (generated[0], generated[1], generated[2], displacement, velocity, memory)
```

```python
import functools

import jax
import jax.numpy as jnp
import numpy as np
from jax import lax
from jax.experimental import pallas as pl
from jax.experimental.pallas import tpu as pltpu
from jax.sharding import PartitionSpec as P

STEPS = 4
TAPS = 64
GLL = 5
SLS = 3
COMP = 5
LANES = 128
TILE = 8
COLS = GLL * GLL
ROWS = COLS * TILE
time_step = 0.04
f32 = jnp.float32
bf16 = jnp.bfloat16

VM = pl.BlockSpec(memory_space=pltpu.VMEM)
SM = pl.BlockSpec(memory_space=pltpu.SMEM)
HB = pl.BlockSpec(memory_space=pl.ANY)


def gll_tables():
    points = np.array([-1.0, -np.sqrt(3.0 / 7.0), 0.0, np.sqrt(3.0 / 7.0), 1.0])
    weights = np.array([0.1, 49.0 / 90.0, 32.0 / 45.0, 49.0 / 90.0, 0.1])
    number = points.shape[0]
    products = np.array(
        [
            np.prod([points[t] - points[o] for o in range(number) if o != t])
            for t in range(number)
        ]
    )
    derivative = np.zeros((number, number))
    for t in range(number):
        for s in range(number):
            if t == s:
                derivative[t, s] = np.sum(
                    [1.0 / (points[t] - points[o]) for o in range(number) if o != t]
                )
            else:
                derivative[t, s] = products[t] / products[s] / (points[t] - points[s])
    return derivative, weights


DMAT, WEIGHTS = gll_tables()
NODE_W = [0.2, 49.0 / 90.0, 32.0 / 45.0, 49.0 / 90.0, 0.2]


def tile_rows(a, b):
    return pl.ds((a * GLL + b) * TILE, TILE)


def at_tile(a, b):
    return pl.ds(pl.multiple_of((a * GLL + b) * TILE, TILE), TILE)


def at_nodes(a, b):
    return pl.ds(pl.multiple_of((a * GLL + b) * TILE, TILE), 4)


def row_index():
    return lax.broadcasted_iota(jnp.int32, (TILE, LANES), 0)


def row_vector(values):
    rows = row_index()
    out = jnp.zeros((TILE, LANES), f32)
    for index, value in enumerate(values):
        out = jnp.where(rows == index, f32(value), out)
    return out


def contract(x, t):
    e0, e1, o0, o1 = x[0] + x[4], x[1] + x[3], x[0] - x[4], x[1] - x[3]

    def odd(p):
        return float((t[p, 0] - t[p, 4]) / 2) * o0 + float((t[p, 1] - t[p, 3]) / 2) * o1

    def even(p):
        return (
            float((t[p, 0] + t[p, 4]) / 2) * e0
            + float((t[p, 1] + t[p, 3]) / 2) * e1
            + float(t[p, 2]) * x[2]
        )

    s0, s1, s2, a0, a1 = odd(0), odd(1), odd(2), even(0), even(1)
    return [s0 + a0, s1 + a1, s2, s1 - a1, s0 - a0]


def permutation(transposed):
    size = 4 * LANES
    first = lax.broadcasted_iota(jnp.int32, (size, size), 0)
    second = lax.broadcasted_iota(jnp.int32, (size, size), 1)
    node, place = (second, first) if transposed else (first, second)
    hit = node == 4 * (place & (LANES - 1)) + (place >> 7)
    return jnp.where(hit, f32(1), f32(0)).astype(bf16)


def exact_dot(x, p):
    high = x.astype(bf16)
    rest = x - high.astype(f32)
    mid = rest.astype(bf16)
    low = (rest - mid.astype(f32)).astype(bf16)
    dot = functools.partial(jnp.dot, preferred_element_type=f32)
    return (dot(low, p) + dot(mid, p)) + dot(high, p)


def call(kernel, outs, in_specs, out_specs=None, scratch=(), aliases=None, name=None):
    return pl.pallas_call(
        kernel,
        out_shape=tuple(jax.ShapeDtypeStruct(o, f32) for o in outs),
        in_specs=in_specs,
        out_specs=out_specs if out_specs is not None else tuple(VM for _ in outs),
        scratch_shapes=list(scratch),
        input_output_aliases=aliases or {},
        name=name,
    )


def load_kernel(gd, gv, cd, cv, den, hist, cells, state, message, x, hrow, sem):
    copies = []
    for base, array in ((0, gd), (3, gv), (6, cd), (9, cv)):
        for a in range(4):
            copies.append(
                pltpu.make_async_copy(
                    array.at[:, a],
                    x.at[pl.ds(base, 3), a // 2, pl.ds(4 * (a % 2), 4), :],
                    sem.at[len(copies)],
                )
            )
    for a in range(4):
        copies.append(
            pltpu.make_async_copy(
                den.at[a], x.at[12, a // 2, pl.ds(4 * (a % 2), 4), :], sem.at[len(copies)]
            )
        )
    copies.append(pltpu.make_async_copy(hist.at[:, 0], hrow, sem.at[len(copies)]))
    for c in copies:
        c.start()
    p = permutation(False)
    for c in copies:
        c.wait()
    y = exact_dot(x[...].reshape(26 * TILE, 4 * LANES), p)
    for m in range(13):
        for a in range(4):
            for c in range(4):
                row = (2 * m + a // 2) * TILE + 4 * (a % 2)
                state[m, pl.ds(a * 40 + c, 4, stride=TILE), :] = y[
                    row : row + 4, c * LANES : (c + 1) * LANES
                ]
    for m in range(13):
        for b in range(4):
            message[m * 4 + b] = state[m, pl.ds(b * TILE, 4), :]
    for k in range(16):
        message[52 + k] = hrow[pl.ds(4 * k, 4), :]
    message[68] = jnp.broadcast_to(cells[0:1, :].astype(f32), (4, LANES))


def load_nodes(gd, gv, cd, cv, den, hist, cells):
    return call(
        load_kernel,
        [(13, ROWS, LANES), (69, 4, LANES)],
        [HB] * 6 + [VM],
        scratch=[
            pltpu.VMEM((13, 2, TILE, 4 * LANES), f32),
            pltpu.VMEM((TAPS, LANES), f32),
            pltpu.SemaphoreType.DMA((21,)),
        ],
        name="load_nodes",
    )(gd, gv, cd, cv, den, hist, cells)


def depth_kernel(state, received, message):
    for m in range(13):
        for a in range(4):
            message[m * 5 + a] = state[m, pl.ds(a * 40, 4), :]
        message[m * 5 + 4] = received[m * 4]


def depth_message(state, received):
    return call(depth_kernel, [(65, 4, LANES)], [VM, VM], name="depth_message")(
        state, received
    )[0]


def filter_kernel(hist, cells, filters, received, out, window):
    count = filters.shape[1]
    table = filters[...]
    high = table.astype(bf16)
    rest = table - high.astype(f32)
    mid = rest.astype(bf16)
    low = (rest - mid.astype(f32)).astype(bf16)
    stack = jnp.concatenate([high, mid, low], axis=0)
    ids = lax.broadcasted_iota(jnp.int32, (count, LANES), 0)
    for k in range(16):
        window[pl.ds(4 * k, 4), :] = received[52 + k]
    for x in range(5):
        if x < 4:
            cell = cells[x : x + 1, :]
            past = hist[:, x, :]
        else:
            cell = received[68][0:1, :].astype(jnp.int32)
            past = window[...]
        one_hot = jnp.where(ids == cell, f32(1), f32(0)).astype(bf16)
        t3 = jnp.dot(stack, one_hot, preferred_element_type=f32)
        taps = (t3[2 * TAPS :] + t3[TAPS : 2 * TAPS]) + t3[:TAPS]
        for lag in range(STEPS):
            kept = TAPS - 1 - lag
            out[lag, pl.ds(x, 1), :] = jnp.sum(
                taps[:kept] * past[lag + 1 :], axis=0, keepdims=True
            )
            out[STEPS + lag, pl.ds(x, 1), :] = taps[TAPS - STEPS + lag : TAPS - STEPS + lag + 1]


def filter_part(hist, cells, filters, received):
    return call(
        filter_kernel,
        [(2 * STEPS, TILE, LANES)],
        [VM] * 4,
        scratch=[pltpu.VMEM((TAPS, LANES), f32)],
        name="filter_part",
    )(hist, cells, filters, received)[0]


def surface_kernel(chunks, top, out, z):
    on_top = top[0]
    for k in range(2 * STEPS):
        for d in range(4):
            z[k, :, pl.ds(d * LANES, LANES)] = chunks[d, k]
    y = exact_dot(z[...].reshape(2 * STEPS * TILE, 4 * LANES), permutation(False))
    keep = on_top > 0
    y = jnp.where(keep, y, f32(0))
    for k in range(2 * STEPS):
        for c in range(4):
            out[k, pl.ds(c, TILE, stride=TILE), :] = y[
                k * TILE : (k + 1) * TILE, c * LANES : (c + 1) * LANES
            ]


def surface_part(chunks, top):
    return call(
        surface_kernel,
        [(2 * STEPS, TILE * TILE, LANES)],
        [VM, SM],
        scratch=[pltpu.VMEM((2 * STEPS, TILE, 4 * LANES), f32)],
        name="surface_part",
    )(chunks, top)[0]


def memory_kernel(gm, cm, lam, mu, dm, kept, memory, sums, moduli, sem):
    copies = []
    for f, array in enumerate((gm, cm)):
        for l in range(SLS):
            copies.append(
                pltpu.make_async_copy(
                    array.at[l, :, :, :, :, 0, 0, :],
                    memory.at[f, l, :, :, :, pl.ds(0, GLL), :],
                    sem.at[len(copies)],
                )
            )
    for index, array in enumerate((lam, mu, dm)):
        copies.append(
            pltpu.make_async_copy(
                array.at[:, :, :, 0, 0, :],
                moduli.at[index, :, :, pl.ds(0, GLL), :],
                sem.at[len(copies)],
            )
        )
    for c in copies:
        c.start()
    for c in copies:
        c.wait()
    wz = row_vector(WEIGHTS)
    for a in range(GLL):
        for b in range(GLL):
            w = wz * float(WEIGHTS[a] * WEIGHTS[b])
            shear = moduli[1, a, b] * w
            moduli[0, a, b] = moduli[0, a, b] * w
            moduli[1, a, b] = shear
            moduli[2, a, b] = moduli[2, a, b] * (2.0 * shear)

    def body(k, carry):
        for f in range(2):
            for a in range(GLL):
                for b in range(GLL):
                    w = wz * float(WEIGHTS[a] * WEIGHTS[b])
                    total = (memory[f, 0, k, a, b] + memory[f, 1, k, a, b]) + memory[f, 2, k, a, b]
                    sums[f, k, pl.ds((a * GLL + b) * TILE, TILE), :] = total * w
        return carry

    lax.fori_loop(0, COMP, body, 0)


def memory_part(gm, cm, lam, mu, dm, kept):
    return call(
        memory_kernel,
        [
            (2, SLS, COMP, GLL, GLL, TILE, LANES),
            (2, COMP, ROWS, LANES),
            (3, GLL, GLL, TILE, LANES),
        ],
        [HB] * 5 + [SM],
        scratch=[pltpu.SemaphoreType.DMA((9,))],
        name="memory_part",
    )(gm, cm, lam, mu, dm, kept)


def sums_kernel(step, kept, memory, *refs):
    strains, sums = refs[:-1], refs[-1]
    k = [kept[l] for l in range(SLS)]

    def power(value, n):
        out = value
        for _ in range(n - 1):
            out = out * value
        return out

    grow = [power(k[l], step) for l in range(SLS)]
    past = []
    for s in range(step):
        n = step - 1 - s
        total = None
        for l in range(SLS):
            term = (1.0 - k[l]) * power(k[l], n) if n else 1.0 - k[l]
            total = term if total is None else total + term
        past.append(total)
    wz = row_vector(WEIGHTS)
    scaled = [[wz * grow[l] for l in range(SLS)]][0]

    def body(j, carry):
        for f in range(2):
            for a in range(GLL):
                for b in range(GLL):
                    here = pl.ds((a * GLL + b) * TILE, TILE)
                    w = float(WEIGHTS[a] * WEIGHTS[b])
                    total = scaled[0] * memory[f, 0, j, a, b]
                    for l in range(1, SLS):
                        total = total + scaled[l] * memory[f, l, j, a, b]
                    total = total * w
                    for s in range(step):
                        total = total + past[s] * strains[s][f, j, here, :]
                    sums[f, j, here, :] = total
        return carry

    lax.fori_loop(0, COMP, body, 0)


def next_sums(step, kept, memory, strains):
    return call(
        functools.partial(sums_kernel, step),
        [(2, COMP, ROWS, LANES)],
        [SM] + [VM] * (1 + len(strains)),
        name=f"sums_{step}",
    )(kept, memory, *strains)[0]


def final_memory_kernel(kept, memory, q0, q1, q2, q3, gout, cout, out, sem):
    strains = (q0, q1, q2, q3)
    iz = row_vector([1.0 / w for w in WEIGHTS])
    coefficients = []
    for l in range(SLS):
        k = kept[l]
        k2 = k * k
        scale = iz * (1.0 - k)
        coefficients.append((k2 * k2, [scale * (k2 * k), scale * k2, scale * k, scale]))

    copies = []
    for f, target in enumerate((gout, cout)):

        def body(j, carry, f=f):
            for a in range(GLL):
                for b in range(GLL):
                    here = pl.ds((a * GLL + b) * TILE, TILE)
                    iw = float(1.0 / (WEIGHTS[a] * WEIGHTS[b]))
                    q = [s[f, j, here, :] * iw for s in strains]
                    for l in range(SLS):
                        decay, cs = coefficients[l]
                        out[f, l, j, a, b] = decay * memory[f, l, j, a, b] + (
                            (cs[0] * q[0] + cs[1] * q[1]) + (cs[2] * q[2] + cs[3] * q[3])
                        )
            return carry

        lax.fori_loop(0, COMP, body, 0)
        for l in range(SLS):
            copy = pltpu.make_async_copy(
                out.at[f, l, :, :, :, pl.ds(0, GLL), :],
                target.at[l, :, :, :, :, 0, 0, :],
                sem.at[len(copies)],
            )
            copy.start()
            copies.append(copy)
    for c in copies:
        c.wait()


def final_memory(kept, memory, strains, shape):
    return call(
        final_memory_kernel,
        [shape, shape],
        [SM] + [VM] * 5,
        out_specs=(HB, HB),
        scratch=[
            pltpu.VMEM((2, SLS, COMP, GLL, GLL, TILE, LANES), f32),
            pltpu.SemaphoreType.DMA((6,)),
        ],
        name="final_memory",
    )(kept, memory, *strains)


def forces(f, u, moduli, sums, grad, stress, force, strain):
    dz = [row_vector(DMAT[:, q]) for q in range(GLL)]
    tz = [row_vector(DMAT[p, :]) for p in range(GLL)]
    rows = row_index()
    for i in range(3):
        for b in range(GLL):
            out = contract([u[f, i, tile_rows(a, b), :] for a in range(GLL)], DMAT)
            for a in range(GLL):
                grad[i, tile_rows(a, b), :] = out[a]
        for a in range(GLL):
            out = contract([u[f, i, tile_rows(a, b), :] for b in range(GLL)], DMAT)
            for b in range(GLL):
                grad[3 + i, tile_rows(a, b), :] = out[b]
    for a in range(GLL):
        for b in range(GLL):
            here = tile_rows(a, b)
            gz = []
            for i in range(3):
                total = None
                for q in range(GLL):
                    row = u[f, i, pl.ds((a * GLL + b) * TILE + q, TILE, stride=0), :]
                    total = dz[q] * row if total is None else total + dz[q] * row
                gz.append(total)
            gx = [grad[i, here, :] for i in range(3)]
            gy = [grad[3 + i, here, :] for i in range(3)]
            lam, mu, dm = moduli[0, a, b], moduli[1, a, b], moduli[2, a, b]
            s = [sums[f, j, here, :] for j in range(COMP)]
            exx, eyy, ezz = gx[0], gy[1], gz[2]
            hxy, hxz, hyz = gy[0] + gx[1], gz[0] + gx[2], gz[1] + gy[2]
            volume = exx + eyy + ezz
            third = volume * f32(1.0 / 3.0)
            mu2 = mu + mu
            pressure = lam * volume
            half = dm * f32(0.5)
            strain[f, 0, here, :] = dm * (exx - third)
            strain[f, 1, here, :] = dm * (eyy - third)
            strain[f, 2, here, :] = half * hxy
            strain[f, 3, here, :] = half * hxz
            strain[f, 4, here, :] = half * hyz
            stress[0, here, :] = pressure + mu2 * exx - s[0]
            stress[1, here, :] = pressure + mu2 * eyy - s[1]
            stress[2, here, :] = pressure + mu2 * ezz + (s[0] + s[1])
            stress[3, here, :] = mu * hxy - s[2]
            stress[4, here, :] = mu * hxz - s[3]
            stress[5, here, :] = mu * hyz - s[4]
    along = ((0, 3, 4), (3, 1, 5), (4, 5, 2))
    for i in range(3):
        for b in range(GLL):
            out = contract(
                [stress[along[0][i], tile_rows(a, b), :] for a in range(GLL)], DMAT.T
            )
            for a in range(GLL):
                grad[i, tile_rows(a, b), :] = out[a]
    for i in range(3):
        for a in range(GLL):
            out = contract(
                [stress[along[1][i], tile_rows(a, b), :] for b in range(GLL)], DMAT.T
            )
            for b in range(GLL):
                here = tile_rows(a, b)
                total = out[b] + grad[i, here, :]
                for p in range(GLL):
                    row = stress[
                        along[2][i], pl.ds((a * GLL + b) * TILE + p, TILE, stride=0), :
                    ]
                    total = total + tz[p] * row
                carried = pltpu.roll(pltpu.roll(total, 1, 1), 4, 0)
                force[f, i, here, :] = total + jnp.where(rows == 0, carried, f32(0))


def face_messages(f, parity, force, first, second):
    par = parity[0]
    high, low = 4 * (1 - par), 4 * par
    for i in range(3):
        for a in range(GLL):
            first[f, i, a] = force[f, i, at_nodes(a, high), :]
            second[f, i, a] = force[f, i, at_nodes(a, low), :]


def with_end_row(x, rows):
    return jnp.where(rows == 4, pltpu.roll(pltpu.roll(x, LANES - 1, 1), 4, 0), x)


def first_kernel(
    state, rx, ry, flags, moduli, sums, u, v, inv, force, strain, first, second, grad, stress
):
    rows = row_index()
    top, bottom = flags[1] > 0, flags[2] > 0
    wz = row_vector(NODE_W)

    def node(m, a, b, tmp):
        if b == 4:
            return ry[m * 5 + a]
        if a == 4:
            return rx[m * 4 + b]
        return state[m, pl.ds((a * GLL + b) * TILE, 4), :]

    for a in range(GLL):
        for b in range(GLL):
            here = pl.ds((a * GLL + b) * TILE, 4)
            inv[here, :] = node(12, a, b, None)
    for a in range(GLL):
        for b in range(GLL):
            here = tile_rows(a, b)
            wy = f32(NODE_W[b])
            if b == 0:
                wy = jnp.where(top, f32(0.1), wy)
            mass = inv[here, :] * (wz * (wy * f32(NODE_W[a])))
            value = f32(time_step) / mass
            if b == 4:
                value = jnp.where(bottom, f32(0), value)
            inv[here, :] = value
    for f in range(2):
        for i in range(3):
            for a in range(GLL):
                for b in range(GLL):
                    here = tile_rows(a, b)
                    four = pl.ds((a * GLL + b) * TILE, 4)
                    u[f, i, four, :] = node(6 * f + i, a, b, None)
                    v[f, i, four, :] = node(6 * f + 3 + i, a, b, None)
    for f in range(2):
        for i in range(3):
            for a in range(GLL):
                for b in range(GLL):
                    here = tile_rows(a, b)
                    u[f, i, here, :] = with_end_row(u[f, i, here, :], rows)

    def body(f, carry):
        forces(f, u, moduli, sums, grad, stress, force, strain)
        face_messages(f, flags, force, first, second)
        return carry

    lax.fori_loop(0, 2, body, 0)


STATE = (2, 3, ROWS, LANES)
FACE = (2, 3, GLL, 4, LANES)
EDGE = (2, 3, 2, GLL * TILE, LANES)
FACES = pltpu.VMEM((3, 2, GLL * TILE, LANES), f32)
WORK = [pltpu.VMEM((6, ROWS, LANES), f32), pltpu.VMEM((6, ROWS, LANES), f32)]


def first_step(state, rx, ry, flags, moduli, sums):
    return call(
        first_kernel,
        [STATE, STATE, (ROWS, LANES), STATE, (2, COMP, ROWS, LANES), FACE, FACE],
        [VM, VM, VM, SM, VM, VM],
        scratch=WORK,
        name="step_0",
    )(state, rx, ry, flags, moduli, sums)


def advance(
    f, step, u_in, v_in, inv, force, edge, xa, xb, flags, surface, samples, u, v, sample_out, face
):
    rows = row_index()
    par = flags[3]
    high, low = 4 * (1 - par), 4 * par
    for i in range(3):
        for b in range(GLL):
            for a, slot, got in ((high, 1 - par, xa), (low, par, xb)):
                if b in (0, 4):
                    row = pl.multiple_of(a * TILE, TILE)
                    own = edge[f, i, b // 4, pl.ds(row, 4), :]
                else:
                    own = force[f, i, at_nodes(a, b), :]
                face[i, slot, pl.ds(b * TILE, 4), :] = own + got[f, i, b]
    for i in range(3):
        for a in range(GLL):
            for b in range(GLL):
                here = tile_rows(a, b)
                scale = inv[here, :]
                if a in (0, 4):
                    total = face[i, a // 4, pl.ds(b * TILE, TILE), :]
                elif b in (0, 4):
                    total = edge[f, i, b // 4, pl.ds(a * TILE, TILE), :]
                else:
                    total = force[f, i, here, :]
                if f == 1 and i == 1 and b == 0:
                    four = pl.ds(a * TILE, TILE)
                    forcing = surface[step, four, :]
                    for s in range(step):
                        forcing = forcing + surface[STEPS + STEPS - 1 - step + s, four, :] * samples[s][a]
                    forcing = forcing + surface[STEPS + STEPS - 1, four, :] * sample_out[a]
                    total = total - forcing
                velocity = v_in[f, i, here, :] - scale * total
                v[f, i, here, :] = velocity
                value = u_in[f, i, here, :] + f32(time_step) * velocity
                value = with_end_row(value, rows)
                u[f, i, here, :] = value
                if f == 0 and i == 1 and b == 0:
                    sample_out[a] = value


def step_kernel(step, u_in, v_in, inv, force_in, edge, xa, xb, flags, surface, moduli, sums, *refs):
    samples, refs = refs[: step - 1], refs[step - 1 :]
    u, v, force, strain, first, second, sample_out, grad, stress, face = refs
    for f in range(2):
        advance(
            f, step - 1, u_in, v_in, inv, force_in, edge, xa, xb, flags, surface, samples, u, v,
            sample_out, face,
        )

    def body(f, carry):
        forces(f, u, moduli, sums, grad, stress, force, strain)
        face_messages(f, flags, force, first, second)
        return carry

    lax.fori_loop(0, 2, body, 0)


def next_step(step, u, v, inv, force, edge, xa, xb, flags, surface, moduli, sums, samples):
    return call(
        functools.partial(step_kernel, step),
        [STATE, STATE, STATE, (2, COMP, ROWS, LANES), FACE, FACE, (GLL, TILE, LANES)],
        [VM] * 7 + [SM] + [VM] * (3 + len(samples)),
        scratch=WORK + [FACES],
        name=f"step_{step}",
    )(u, v, inv, force, edge, xa, xb, flags, surface, moduli, sums, *samples)


def fold_kernel(force, ya, yb, flags, edge, first, second):
    pd, ps = flags[0], flags[3]
    for f in range(2):
        for i in range(3):
            for slot, b, got in ((1 - pd, 4 * (1 - pd), ya), (pd, 4 * pd, yb)):
                for a in range(GLL):
                    edge[f, i, slot, pl.ds(a * TILE, 4), :] = (
                        force[f, i, at_nodes(a, b), :] + got[f, i, a]
                    )
            for out, a in ((first, 4 * (1 - ps)), (second, 4 * ps)):
                for b in range(GLL):
                    if b in (0, 4):
                        row = pl.multiple_of(a * TILE, TILE)
                        out[f, i, b] = edge[f, i, b // 4, pl.ds(row, 4), :]
                    else:
                        out[f, i, b] = force[f, i, at_nodes(a, b), :]


def fold_depth(force, ya, yb, flags):
    return call(
        fold_kernel,
        [EDGE, FACE, FACE],
        [VM, VM, VM, SM],
        name="fold_depth",
    )(force, ya, yb, flags)


def finish_kernel(
    u_in, v_in, inv, force, edge, xa, xb, flags, surface, s0, s1, s2, gd, gv, cd, cv, u, v, last, face,
    z, sem
):
    for f in range(2):
        advance(
            f, STEPS - 1, u_in, v_in, inv, force, edge, xa, xb, flags, surface, (s0, s1, s2), u, v,
            last, face,
        )
    for f in range(2):
        for kind, array in enumerate((u, v)):
            for i in range(3):
                m = (f * 2 + kind) * 3 + i
                for a in range(4):
                    for c in range(4):
                        z[m, a // 2, pl.ds(4 * (a % 2), 4), pl.ds(c * LANES, LANES)] = array[
                            f, i, pl.ds(a * 40 + c, 4, stride=TILE), :
                        ]
    out = exact_dot(z[...].reshape(24 * TILE, 4 * LANES), permutation(True))
    z[...] = out.reshape(12, 2, TILE, 4 * LANES)
    copies = []
    for k, target in enumerate((gd, gv, cd, cv)):
        for a in range(4):
            copy = pltpu.make_async_copy(
                z.at[pl.ds(3 * k, 3), a // 2, pl.ds(4 * (a % 2), 4), :],
                target.at[:, a],
                sem.at[len(copies)],
            )
            copy.start()
            copies.append(copy)
    for c in copies:
        c.wait()


def finish(u, v, inv, force, edge, xa, xb, flags, surface, samples, shape):
    return call(
        finish_kernel,
        [shape] * 4,
        [VM] * 7 + [SM] + [VM] * 4,
        out_specs=(HB,) * 4,
        scratch=[
            pltpu.VMEM(STATE, f32),
            pltpu.VMEM(STATE, f32),
            pltpu.VMEM((GLL, TILE, LANES), f32),
            FACES,
            pltpu.VMEM((12, 2, TILE, 4 * LANES), f32),
            pltpu.SemaphoreType.DMA((16,)),
        ],
        name="finish",
    )(u, v, inv, force, edge, xa, xb, flags, surface, *samples)


def ring(value, axis, steps):
    count = lax.axis_size(axis)
    return lax.ppermute(value, axis, [(s, (s + steps) % count) for s in range(count)])


def up(value, axis):
    count = lax.axis_size(axis)
    return lax.ppermute(value, axis, [(s, s - 1) for s in range(1, count)])


def swap(value, axis, offset, periodic):
    count = lax.axis_size(axis)
    pairs = []
    for s in range(offset, count, 2):
        t = s + 1
        if t == count:
            if not periodic:
                continue
            t = 0
        pairs += [(s, t), (t, s)]
    return lax.ppermute(value, axis, pairs)


def gather_top(part):
    count = lax.axis_size("depth")
    held, reach = part[None], 1
    while reach < count:
        pairs = [(d, d - reach) for d in range(reach, count, 2 * reach)]
        held = jnp.concatenate([held, lax.ppermute(held, "depth", pairs)], axis=0)
        reach *= 2
    return held


def body(gd, gv, gm, cd, cv, cm, lam, mu, dm, kept, den, hist, cells, filters):
    slab, depth = lax.axis_index("slab"), lax.axis_index("depth")
    flags = jnp.stack(
        [
            depth % 2,
            (depth == 0).astype(jnp.int32),
            (depth == lax.axis_size("depth") - 1).astype(jnp.int32),
            slab % 2,
        ]
    ).astype(jnp.int32)
    state, message = load_nodes(gd, gv, cd, cv, den, hist, cells)
    rx = ring(message, "slab", -1)
    memory, sums, moduli = memory_part(gm, cm, lam, mu, dm, kept)
    ry = up(depth_message(state, rx), "depth")
    part = filter_part(hist, cells, filters.T, rx)
    surface = surface_part(gather_top(part), flags[1:2])
    u, v, inv, force, strain, first, second = first_step(state, rx, ry, flags, moduli, sums)
    strains, samples = [strain], []
    for step in range(1, STEPS + 1):
        yb = swap(second, "depth", 1, False)
        ya = swap(first, "depth", 0, False)
        edge, first, second = fold_depth(force, ya, yb, flags)
        xb = swap(second, "slab", 1, True)
        xa = swap(first, "slab", 0, True)
        if step < STEPS:
            sums = next_sums(step, kept, memory, strains)
            u, v, force, strain, first, second, sample = next_step(
                step, u, v, inv, force, edge, xa, xb, flags, surface, moduli, sums, samples
            )
            strains.append(strain)
            samples.append(sample)
        else:
            gm_out, cm_out = final_memory(kept, memory, strains, gm.shape)
            gd_out, gv_out, cd_out, cv_out = finish(
                u, v, inv, force, edge, xa, xb, flags, surface, samples, gd.shape
            )
    return gd_out, gv_out, gm_out, cd_out, cv_out, cm_out


def solution(mesh):
    nodes = P(None, "slab", "depth", None)
    memory = P(None, None, None, None, None, "slab", "depth", None)
    points = P(None, None, None, "slab", "depth", None)
    return jax.shard_map(
        body,
        mesh=mesh,
        in_specs=(
            nodes,
            nodes,
            memory,
            nodes,
            nodes,
            memory,
            points,
            points,
            points,
            P(),
            P("slab", "depth", None),
            P(None, "slab", "depth"),
            P("slab", "depth"),
            P(),
        ),
        out_specs=(nodes, nodes, memory, nodes, nodes, memory),
        check_vma=False,
    )
```

```python
import functools

import jax
import jax.numpy as jnp
import numpy as np
from jax import lax
from jax.experimental import pallas as pl
from jax.experimental.pallas import tpu as pltpu
from jax.sharding import PartitionSpec as P

STEPS = 4
TAPS = 64
GLL = 5
SLS = 3
COMP = 5
LANES = 128
TILE = 8
COLS = GLL * GLL
ROWS = COLS * TILE
time_step = 0.04
f32 = jnp.float32
bf16 = jnp.bfloat16

VM = pl.BlockSpec(memory_space=pltpu.VMEM)
SM = pl.BlockSpec(memory_space=pltpu.SMEM)
HB = pl.BlockSpec(memory_space=pltpu.HBM)


def gll_tables():
    points = np.array([-1.0, -np.sqrt(3.0 / 7.0), 0.0, np.sqrt(3.0 / 7.0), 1.0])
    weights = np.array([0.1, 49.0 / 90.0, 32.0 / 45.0, 49.0 / 90.0, 0.1])
    number = points.shape[0]
    products = np.array(
        [
            np.prod([points[t] - points[o] for o in range(number) if o != t])
            for t in range(number)
        ]
    )
    derivative = np.zeros((number, number))
    for t in range(number):
        for s in range(number):
            if t == s:
                derivative[t, s] = np.sum(
                    [1.0 / (points[t] - points[o]) for o in range(number) if o != t]
                )
            else:
                derivative[t, s] = products[t] / products[s] / (points[t] - points[s])
    return derivative, weights


DMAT, WEIGHTS = gll_tables()
NODE_W = [0.2, 49.0 / 90.0, 32.0 / 45.0, 49.0 / 90.0, 0.2]


def tile_rows(a, b):
    return pl.ds((a * GLL + b) * TILE, TILE)


def at_tile(a, b):
    return pl.ds(pl.multiple_of((a * GLL + b) * TILE, TILE), TILE)


def at_nodes(a, b):
    return pl.ds(pl.multiple_of((a * GLL + b) * TILE, TILE), 4)


def row_index():
    return lax.broadcasted_iota(jnp.int32, (TILE, LANES), 0)


def row_vector(values):
    rows = row_index()
    out = jnp.zeros((TILE, LANES), f32)
    for index, value in enumerate(values):
        out = jnp.where(rows == index, f32(value), out)
    return out


def contract(x, t):
    e0, e1, o0, o1 = x[0] + x[4], x[1] + x[3], x[0] - x[4], x[1] - x[3]

    def odd(p):
        return float((t[p, 0] - t[p, 4]) / 2) * o0 + float((t[p, 1] - t[p, 3]) / 2) * o1

    def even(p):
        return (
            float((t[p, 0] + t[p, 4]) / 2) * e0
            + float((t[p, 1] + t[p, 3]) / 2) * e1
            + float(t[p, 2]) * x[2]
        )

    s0, s1, s2, a0, a1 = odd(0), odd(1), odd(2), even(0), even(1)
    return [s0 + a0, s1 + a1, s2, s1 - a1, s0 - a0]


def permutation(transposed):
    size = 4 * LANES
    first = lax.broadcasted_iota(jnp.int32, (size, size), 0)
    second = lax.broadcasted_iota(jnp.int32, (size, size), 1)
    node, place = (second, first) if transposed else (first, second)
    hit = node == 4 * (place & (LANES - 1)) + (place >> 7)
    return jnp.where(hit, f32(1), f32(0)).astype(bf16)


def exact_dot(x, p):
    high = x.astype(bf16)
    rest = x - high.astype(f32)
    mid = rest.astype(bf16)
    low = (rest - mid.astype(f32)).astype(bf16)
    dot = functools.partial(jnp.dot, preferred_element_type=f32)
    return (dot(low, p) + dot(mid, p)) + dot(high, p)


def call(kernel, outs, in_specs, out_specs=None, scratch=(), aliases=None, name=None, limit=10):
    run = pl.pallas_call(
        kernel,
        out_shape=tuple(
            pltpu.VMEM(o, f32) if out_specs is None else jax.ShapeDtypeStruct(o, f32) for o in outs
        ),
        in_specs=in_specs,
        out_specs=out_specs if out_specs is not None else tuple(VM for _ in outs),
        scratch_shapes=list(scratch),
        input_output_aliases=aliases or {},
        name=name,
        compiler_params=pltpu.CompilerParams(vmem_limit_bytes=limit << 20),
    )

    def placed(*operands):
        spaces = {id(VM): pltpu.VMEM, id(HB): pltpu.HBM}
        return run(
            *(
                pltpu.with_memory_space_constraint(o, spaces[id(s)]) if id(s) in spaces else o
                for o, s in zip(operands, in_specs)
            )
        )

    return placed


def load_kernel(gd, gv, cd, cv, den, hist, cells, flags, state, message, x, hrow, crow, sem):
    copies = []
    for base, array in ((0, gd), (3, gv), (6, cd), (9, cv)):
        for a in range(4):
            copies.append(
                pltpu.make_async_copy(
                    array.at[:, a],
                    x.at[pl.ds(base, 3), a // 2, pl.ds(4 * (a % 2), 4), :],
                    sem.at[len(copies)],
                )
            )
    for a in range(4):
        copies.append(
            pltpu.make_async_copy(
                den.at[a], x.at[12, a // 2, pl.ds(4 * (a % 2), 4), :], sem.at[len(copies)]
            )
        )
    copies.append(pltpu.make_async_copy(hist.at[:, 0], hrow, sem.at[len(copies)]))
    copies.append(pltpu.make_async_copy(cells, crow, sem.at[len(copies)]))
    for c in copies:
        c.start()
    p = permutation(False)
    for c in copies:
        c.wait()
    y = exact_dot(x[...].reshape(26 * TILE, 4 * LANES), p)
    for m in range(13):
        for a in range(4):
            for c in range(4):
                row = (2 * m + a // 2) * TILE + 4 * (a % 2)
                state[m, pl.ds(a * 40 + c, 4, stride=TILE), :] = y[
                    row : row + 4, c * LANES : (c + 1) * LANES
                ]
    for m in range(13):
        for b in range(4):
            message[m * 4 + b] = state[m, pl.ds(b * TILE, 4), :]
    for k in range(16):
        message[52 + k] = hrow[pl.ds(4 * k, 4), :]
    message[68] = jnp.broadcast_to(crow[0:1, :].astype(f32), (4, LANES))


def load_nodes(gd, gv, cd, cv, den, hist, cells, flags):
    return call(
        load_kernel,
        [(13, ROWS, LANES), (69, 4, LANES)],
        [HB] * 7 + [SM],
        scratch=[
            pltpu.VMEM((13, 2, TILE, 4 * LANES), f32),
            pltpu.VMEM((TAPS, LANES), f32),
            pltpu.VMEM((4, LANES), jnp.int32),
            pltpu.SemaphoreType.DMA((22,)),
        ],
        name="load_nodes",
    )(gd, gv, cd, cv, den, hist, cells, flags)


def depth_kernel(state, received, after, message):
    for m in range(13):
        for a in range(4):
            message[m * 5 + a] = state[m, pl.ds(a * 40, 4), :]
        message[m * 5 + 4] = received[m * 4]


def depth_message(state, received, after):
    return call(depth_kernel, [(65, 4, LANES)], [VM] * 3, name="depth_message")(
        state, received, after
    )[0]


def filter_kernel(hist_in, cells_in, filters_in, received, after, out, window, hist, cells, filters, sem):
    copies = []
    for source, target in ((hist_in, hist), (cells_in, cells), (filters_in, filters)):
        copies.append(pltpu.make_async_copy(source, target, sem.at[len(copies)]))
        copies[-1].start()
    for c in copies:
        c.wait()
    count = filters.shape[1]
    table = filters[...]
    high = table.astype(bf16)
    rest = table - high.astype(f32)
    mid = rest.astype(bf16)
    low = (rest - mid.astype(f32)).astype(bf16)
    stack = jnp.concatenate([high, mid, low], axis=0)
    ids = lax.broadcasted_iota(jnp.int32, (count, LANES), 0)
    for k in range(16):
        window[pl.ds(4 * k, 4), :] = received[52 + k]
    for x in range(5):
        if x < 4:
            cell = cells[x : x + 1, :]
            past = hist[:, x, :]
        else:
            cell = received[68][0:1, :].astype(jnp.int32)
            past = window[...]
        one_hot = jnp.where(ids == cell, f32(1), f32(0)).astype(bf16)
        t3 = jnp.dot(stack, one_hot, preferred_element_type=f32)
        taps = (t3[2 * TAPS :] + t3[TAPS : 2 * TAPS]) + t3[:TAPS]
        for lag in range(STEPS):
            kept = TAPS - 1 - lag
            out[lag, pl.ds(x, 1), :] = jnp.sum(
                taps[:kept] * past[lag + 1 :], axis=0, keepdims=True
            )
            out[STEPS + lag, pl.ds(x, 1), :] = taps[TAPS - STEPS + lag : TAPS - STEPS + lag + 1]


def filter_part(hist, cells, filters, received, after):
    return call(
        filter_kernel,
        [(2 * STEPS, TILE, LANES)],
        [HB] * 3 + [VM] * 2,
        scratch=[
            pltpu.VMEM((TAPS, LANES), f32),
            pltpu.VMEM(hist.shape, f32),
            pltpu.VMEM(cells.shape, jnp.int32),
            pltpu.VMEM(filters.shape, f32),
            pltpu.SemaphoreType.DMA((3,)),
        ],
        name="filter_part",
    )(hist, cells, filters, received, after)[0]


def join_kernel(mine, other, after, out):
    half = out.shape[0] // 2
    out[pl.ds(0, half)] = mine[...]
    out[pl.ds(half, half)] = other[...]


def join(mine, other, after):
    return call(
        join_kernel, [(2 * mine.shape[0],) + mine.shape[1:]], [VM] * 3, name="join"
    )(mine, other, after)[0]


def surface_kernel(chunks, top, out, z):
    on_top = top[0]
    for k in range(2 * STEPS):
        for d in range(4):
            z[k, :, pl.ds(d * LANES, LANES)] = chunks[d, k]
    y = exact_dot(z[...].reshape(2 * STEPS * TILE, 4 * LANES), permutation(False))
    keep = on_top > 0
    y = jnp.where(keep, y, f32(0))
    for k in range(2 * STEPS):
        for c in range(4):
            out[k, pl.ds(c, TILE, stride=TILE), :] = y[
                k * TILE : (k + 1) * TILE, c * LANES : (c + 1) * LANES
            ]


def surface_part(chunks, top):
    return call(
        surface_kernel,
        [(2 * STEPS, TILE * TILE, LANES)],
        [VM, SM],
        scratch=[pltpu.VMEM((2 * STEPS, TILE, 4 * LANES), f32)],
        name="surface_part",
    )(chunks, top)[0]


def memory_kernel(gm, cm, lam, mu, dm, memory, sums, moduli, sem):
    copies = []
    for f, array in enumerate((gm, cm)):
        for l in range(SLS):
            copies.append(
                pltpu.make_async_copy(
                    array.at[l, :, :, :, :, 0, 0, :],
                    memory.at[f, l, :, :, :, pl.ds(0, GLL), :],
                    sem.at[len(copies)],
                )
            )
    for index, array in enumerate((lam, mu, dm)):
        copies.append(
            pltpu.make_async_copy(
                array.at[:, :, :, 0, 0, :],
                moduli.at[index, :, :, pl.ds(0, GLL), :],
                sem.at[len(copies)],
            )
        )
    for c in copies:
        c.start()
    for c in copies:
        c.wait()
    wz = row_vector(WEIGHTS)
    for a in range(GLL):
        for b in range(GLL):
            w = wz * float(WEIGHTS[a] * WEIGHTS[b])
            shear = moduli[1, a, b] * w
            moduli[0, a, b] = moduli[0, a, b] * w
            moduli[1, a, b] = shear
            moduli[2, a, b] = moduli[2, a, b] * (2.0 * shear)

    def body(k, carry):
        for f in range(2):
            for a in range(GLL):
                for b in range(GLL):
                    w = wz * float(WEIGHTS[a] * WEIGHTS[b])
                    total = (memory[f, 0, k, a, b] + memory[f, 1, k, a, b]) + memory[f, 2, k, a, b]
                    sums[f, k, pl.ds((a * GLL + b) * TILE, TILE), :] = total * w
        return carry

    lax.fori_loop(0, COMP, body, 0)


def memory_part(gm, cm, lam, mu, dm):
    return call(
        memory_kernel,
        [
            (2, SLS, COMP, GLL, GLL, TILE, LANES),
            (2, COMP, ROWS, LANES),
            (3, GLL, GLL, TILE, LANES),
        ],
        [HB] * 5,
        scratch=[pltpu.SemaphoreType.DMA((9,))],
        name="memory_part",
    )(gm, cm, lam, mu, dm)


def sums_kernel(step, kept, memory, *refs):
    strains, sums = refs[:-1], refs[-1]
    k = [kept[l] for l in range(SLS)]

    def power(value, n):
        out = value
        for _ in range(n - 1):
            out = out * value
        return out

    grow = [power(k[l], step) for l in range(SLS)]
    past = []
    for s in range(step):
        n = step - 1 - s
        total = None
        for l in range(SLS):
            term = (1.0 - k[l]) * power(k[l], n) if n else 1.0 - k[l]
            total = term if total is None else total + term
        past.append(total)
    wz = row_vector(WEIGHTS)
    scaled = [[wz * grow[l] for l in range(SLS)]][0]

    def body(j, carry):
        for f in range(2):
            for a in range(GLL):
                for b in range(GLL):
                    here = pl.ds((a * GLL + b) * TILE, TILE)
                    w = float(WEIGHTS[a] * WEIGHTS[b])
                    total = scaled[0] * memory[f, 0, j, a, b]
                    for l in range(1, SLS):
                        total = total + scaled[l] * memory[f, l, j, a, b]
                    total = total * w
                    for s in range(step):
                        total = total + past[s] * strains[s][f, j, here, :]
                    sums[f, j, here, :] = total
        return carry

    lax.fori_loop(0, COMP, body, 0)


def next_sums(step, kept, memory, strains):
    return call(
        functools.partial(sums_kernel, step),
        [(2, COMP, ROWS, LANES)],
        [SM] + [VM] * (1 + len(strains)),
        name=f"sums_{step}",
    )(kept, memory, *strains)[0]


def final_memory_kernel(kept, memory, q0, q1, q2, q3, gout, cout, out, sem):
    strains = (q0, q1, q2, q3)
    iz = row_vector([1.0 / w for w in WEIGHTS])
    coefficients = []
    for l in range(SLS):
        k = kept[l]
        k2 = k * k
        scale = iz * (1.0 - k)
        coefficients.append((k2 * k2, [scale * (k2 * k), scale * k2, scale * k, scale]))

    copies = []
    for f, target in enumerate((gout, cout)):

        def body(j, carry, f=f):
            for a in range(GLL):
                for b in range(GLL):
                    here = pl.ds((a * GLL + b) * TILE, TILE)
                    iw = float(1.0 / (WEIGHTS[a] * WEIGHTS[b]))
                    q = [s[f, j, here, :] * iw for s in strains]
                    for l in range(SLS):
                        decay, cs = coefficients[l]
                        out[f, l, j, a, b] = decay * memory[f, l, j, a, b] + (
                            (cs[0] * q[0] + cs[1] * q[1]) + (cs[2] * q[2] + cs[3] * q[3])
                        )
            return carry

        lax.fori_loop(0, COMP, body, 0)
        for l in range(SLS):
            copy = pltpu.make_async_copy(
                out.at[f, l, :, :, :, pl.ds(0, GLL), :],
                target.at[l, :, :, :, :, 0, 0, :],
                sem.at[len(copies)],
            )
            copy.start()
            copies.append(copy)
    for c in copies:
        c.wait()


def final_memory(kept, memory, strains, shape):
    return call(
        final_memory_kernel,
        [shape, shape],
        [SM] + [VM] * 5,
        out_specs=(HB, HB),
        scratch=[
            pltpu.VMEM((2, SLS, COMP, GLL, GLL, TILE, LANES), f32),
            pltpu.SemaphoreType.DMA((6,)),
        ],
        name="final_memory",
    )(kept, memory, *strains)


def forces(f, u, moduli, sums, grad, stress, force, strain):
    dz = [row_vector(DMAT[:, q]) for q in range(GLL)]
    tz = [row_vector(DMAT[p, :]) for p in range(GLL)]
    rows = row_index()
    for i in range(3):
        for b in range(GLL):
            out = contract([u[f, i, tile_rows(a, b), :] for a in range(GLL)], DMAT)
            for a in range(GLL):
                grad[i, tile_rows(a, b), :] = out[a]
        for a in range(GLL):
            out = contract([u[f, i, tile_rows(a, b), :] for b in range(GLL)], DMAT)
            for b in range(GLL):
                grad[3 + i, tile_rows(a, b), :] = out[b]
    for a in range(GLL):
        for b in range(GLL):
            here = tile_rows(a, b)
            gz = []
            for i in range(3):
                total = None
                for q in range(GLL):
                    row = u[f, i, pl.ds((a * GLL + b) * TILE + q, TILE, stride=0), :]
                    total = dz[q] * row if total is None else total + dz[q] * row
                gz.append(total)
            gx = [grad[i, here, :] for i in range(3)]
            gy = [grad[3 + i, here, :] for i in range(3)]
            lam, mu, dm = moduli[0, a, b], moduli[1, a, b], moduli[2, a, b]
            s = [sums[f, j, here, :] for j in range(COMP)]
            exx, eyy, ezz = gx[0], gy[1], gz[2]
            hxy, hxz, hyz = gy[0] + gx[1], gz[0] + gx[2], gz[1] + gy[2]
            volume = exx + eyy + ezz
            third = volume * f32(1.0 / 3.0)
            mu2 = mu + mu
            pressure = lam * volume
            half = dm * f32(0.5)
            strain[f, 0, here, :] = dm * (exx - third)
            strain[f, 1, here, :] = dm * (eyy - third)
            strain[f, 2, here, :] = half * hxy
            strain[f, 3, here, :] = half * hxz
            strain[f, 4, here, :] = half * hyz
            stress[0, here, :] = pressure + mu2 * exx - s[0]
            stress[1, here, :] = pressure + mu2 * eyy - s[1]
            stress[2, here, :] = pressure + mu2 * ezz + (s[0] + s[1])
            stress[3, here, :] = mu * hxy - s[2]
            stress[4, here, :] = mu * hxz - s[3]
            stress[5, here, :] = mu * hyz - s[4]
    along = ((0, 3, 4), (3, 1, 5), (4, 5, 2))
    for i in range(3):
        for b in range(GLL):
            out = contract(
                [stress[along[0][i], tile_rows(a, b), :] for a in range(GLL)], DMAT.T
            )
            for a in range(GLL):
                grad[i, tile_rows(a, b), :] = out[a]
    for i in range(3):
        for a in range(GLL):
            out = contract(
                [stress[along[1][i], tile_rows(a, b), :] for b in range(GLL)], DMAT.T
            )
            for b in range(GLL):
                here = tile_rows(a, b)
                total = out[b] + grad[i, here, :]
                for p in range(GLL):
                    row = stress[
                        along[2][i], pl.ds((a * GLL + b) * TILE + p, TILE, stride=0), :
                    ]
                    total = total + tz[p] * row
                carried = pltpu.roll(pltpu.roll(total, 1, 1), 4, 0)
                force[f, i, here, :] = total + jnp.where(rows == 0, carried, f32(0))


def face_messages(f, parity, force, first, second):
    par = parity[0]
    high, low = 4 * (1 - par), 4 * par
    for i in range(3):
        for a in range(GLL):
            first[f, i, a] = force[f, i, at_nodes(a, high), :]
            second[f, i, a] = force[f, i, at_nodes(a, low), :]


def with_end_row(x, rows):
    return jnp.where(rows == 4, pltpu.roll(pltpu.roll(x, LANES - 1, 1), 4, 0), x)


def first_kernel(
    state, rx, ry, flags, moduli, sums, u, v, inv, force, strain, first, second, grad, stress
):
    rows = row_index()
    top, bottom = flags[1] > 0, flags[2] > 0
    wz = row_vector(NODE_W)

    def node(m, a, b, tmp):
        if b == 4:
            if m == 12:
                return ry[m * 5 + a]
            return jnp.where(bottom, f32(0), ry[m * 5 + a])
        if a == 4:
            return rx[m * 4 + b]
        return state[m, pl.ds((a * GLL + b) * TILE, 4), :]

    for a in range(GLL):
        for b in range(GLL):
            here = pl.ds((a * GLL + b) * TILE, 4)
            inv[here, :] = node(12, a, b, None)
    for a in range(GLL):
        for b in range(GLL):
            here = tile_rows(a, b)
            wy = f32(NODE_W[b])
            if b == 0:
                wy = jnp.where(top, f32(0.1), wy)
            mass = inv[here, :] * (wz * (wy * f32(NODE_W[a])))
            value = f32(time_step) / mass
            if b == 4:
                value = jnp.where(bottom, f32(0), value)
            inv[here, :] = value
    for f in range(2):
        for i in range(3):
            for a in range(GLL):
                for b in range(GLL):
                    here = tile_rows(a, b)
                    four = pl.ds((a * GLL + b) * TILE, 4)
                    u[f, i, four, :] = node(6 * f + i, a, b, None)
                    v[f, i, four, :] = node(6 * f + 3 + i, a, b, None)
    for f in range(2):
        for i in range(3):
            for a in range(GLL):
                for b in range(GLL):
                    here = tile_rows(a, b)
                    u[f, i, here, :] = with_end_row(u[f, i, here, :], rows)

    def body(f, carry):
        forces(f, u, moduli, sums, grad, stress, force, strain)
        face_messages(f, flags, force, first, second)
        return carry

    lax.fori_loop(0, 2, body, 0)


STATE = (2, 3, ROWS, LANES)
FACE = (2, 3, GLL, 4, LANES)
EDGE = (2, 3, 2, GLL * TILE, LANES)
FACES = pltpu.VMEM((3, 2, GLL * TILE, LANES), f32)
WORK = [pltpu.VMEM((6, ROWS, LANES), f32), pltpu.VMEM((6, ROWS, LANES), f32)]


def first_step(state, rx, ry, flags, moduli, sums):
    return call(
        first_kernel,
        [STATE, STATE, (ROWS, LANES), STATE, (2, COMP, ROWS, LANES), FACE, FACE],
        [VM, VM, VM, SM, VM, VM],
        scratch=WORK,
        name="step_0",
    )(state, rx, ry, flags, moduli, sums)


def advance(
    f, step, u_in, v_in, inv, force, edge, xa, xb, flags, surface, samples, u, v, sample_out, face
):
    rows = row_index()
    par = flags[3]
    high, low = 4 * (1 - par), 4 * par
    for i in range(3):
        for b in range(GLL):
            for a, slot, got in ((high, 1 - par, xa), (low, par, xb)):
                if b in (0, 4):
                    row = pl.multiple_of(a * TILE, TILE)
                    own = edge[f, i, b // 4, pl.ds(row, 4), :]
                else:
                    own = force[f, i, at_nodes(a, b), :]
                face[i, slot, pl.ds(b * TILE, 4), :] = own + got[f, i, b]
    for i in range(3):
        for a in range(GLL):
            for b in range(GLL):
                here = tile_rows(a, b)
                scale = inv[here, :]
                if a in (0, 4):
                    total = face[i, a // 4, pl.ds(b * TILE, TILE), :]
                elif b in (0, 4):
                    total = edge[f, i, b // 4, pl.ds(a * TILE, TILE), :]
                else:
                    total = force[f, i, here, :]
                if f == 1 and i == 1 and b == 0:
                    four = pl.ds(a * TILE, TILE)
                    forcing = surface[step, four, :]
                    for s in range(step):
                        forcing = forcing + surface[STEPS + STEPS - 1 - step + s, four, :] * samples[s][a]
                    forcing = forcing + surface[STEPS + STEPS - 1, four, :] * sample_out[a]
                    total = total - forcing
                velocity = v_in[f, i, here, :] - scale * total
                v[f, i, here, :] = velocity
                value = u_in[f, i, here, :] + f32(time_step) * velocity
                value = with_end_row(value, rows)
                u[f, i, here, :] = value
                if f == 0 and i == 1 and b == 0:
                    sample_out[a] = value


def step_kernel(step, u_in, v_in, inv, force_in, edge, xa, xb, flags, surface, moduli, sums, *refs):
    samples, refs = refs[: step - 1], refs[step - 1 :]
    u, v, force, strain, first, second, sample_out, grad, stress, face = refs
    for f in range(2):
        advance(
            f, step - 1, u_in, v_in, inv, force_in, edge, xa, xb, flags, surface, samples, u, v,
            sample_out, face,
        )

    def body(f, carry):
        forces(f, u, moduli, sums, grad, stress, force, strain)
        face_messages(f, flags, force, first, second)
        return carry

    lax.fori_loop(0, 2, body, 0)


def next_step(step, u, v, inv, force, edge, xa, xb, flags, surface, moduli, sums, samples):
    return call(
        functools.partial(step_kernel, step),
        [STATE, STATE, STATE, (2, COMP, ROWS, LANES), FACE, FACE, (GLL, TILE, LANES)],
        [VM] * 7 + [SM] + [VM] * (3 + len(samples)),
        scratch=WORK + [FACES],
        name=f"step_{step}",
    )(u, v, inv, force, edge, xa, xb, flags, surface, moduli, sums, *samples)


def fold_kernel(force, ya, yb, flags, edge, first, second):
    pd, ps, top = flags[0], flags[3], flags[1] > 0
    for f in range(2):
        for i in range(3):
            for a in range(GLL):
                here = pl.ds(a * TILE, 4)
                edge[f, i, 1 - pd, here, :] = (
                    force[f, i, at_nodes(a, 4 * (1 - pd)), :] + ya[f, i, a]
                )
                other = jnp.where(top, f32(0), yb[f, i, a])
                edge[f, i, pd, here, :] = force[f, i, at_nodes(a, 4 * pd), :] + other
            for out, a in ((first, 4 * (1 - ps)), (second, 4 * ps)):
                for b in range(GLL):
                    if b in (0, 4):
                        row = pl.multiple_of(a * TILE, TILE)
                        out[f, i, b] = edge[f, i, b // 4, pl.ds(row, 4), :]
                    else:
                        out[f, i, b] = force[f, i, at_nodes(a, b), :]


def fold_depth(force, ya, yb, flags):
    return call(
        fold_kernel,
        [EDGE, FACE, FACE],
        [VM, VM, VM, SM],
        name="fold_depth",
    )(force, ya, yb, flags)


def finish_kernel(
    u_in, v_in, inv, force, edge, xa, xb, flags, surface, s0, s1, s2, gd, gv, cd, cv, u, v, last, face,
    z, sem
):
    for f in range(2):
        advance(
            f, STEPS - 1, u_in, v_in, inv, force, edge, xa, xb, flags, surface, (s0, s1, s2), u, v,
            last, face,
        )
    for f in range(2):
        for kind, array in enumerate((u, v)):
            for i in range(3):
                m = (f * 2 + kind) * 3 + i
                for a in range(4):
                    for c in range(4):
                        z[m, a // 2, pl.ds(4 * (a % 2), 4), pl.ds(c * LANES, LANES)] = array[
                            f, i, pl.ds(a * 40 + c, 4, stride=TILE), :
                        ]
    out = exact_dot(z[...].reshape(24 * TILE, 4 * LANES), permutation(True))
    z[...] = out.reshape(12, 2, TILE, 4 * LANES)
    copies = []
    for k, target in enumerate((gd, gv, cd, cv)):
        for a in range(4):
            copy = pltpu.make_async_copy(
                z.at[pl.ds(3 * k, 3), a // 2, pl.ds(4 * (a % 2), 4), :],
                target.at[:, a],
                sem.at[len(copies)],
            )
            copy.start()
            copies.append(copy)
    for c in copies:
        c.wait()


def finish(u, v, inv, force, edge, xa, xb, flags, surface, samples, shape):
    return call(
        finish_kernel,
        [shape] * 4,
        [VM] * 7 + [SM] + [VM] * 4,
        out_specs=(HB,) * 4,
        scratch=[
            pltpu.VMEM(STATE, f32),
            pltpu.VMEM(STATE, f32),
            pltpu.VMEM((GLL, TILE, LANES), f32),
            FACES,
            pltpu.VMEM((12, 2, TILE, 4 * LANES), f32),
            pltpu.SemaphoreType.DMA((16,)),
        ],
        name="finish",
    )(u, v, inv, force, edge, xa, xb, flags, surface, *samples)


def ring(value, axis, steps):
    count = lax.axis_size(axis)
    return lax.ppermute(value, axis, [(s, (s + steps) % count) for s in range(count)])


def swap(value, axis, offset):
    count = lax.axis_size(axis)
    pairs = []
    for s in range(offset, count + offset, 2):
        pairs += [(s % count, (s + 1) % count), ((s + 1) % count, s % count)]
    return lax.ppermute(value, axis, pairs)


def body(gd, gv, gm, cd, cv, cm, lam, mu, dm, kept, den, hist, cells, filters):
    filters = filters.T
    slab, depth = lax.axis_index("slab"), lax.axis_index("depth")
    flags = jnp.stack(
        [
            depth % 2,
            (depth == 0).astype(jnp.int32),
            (depth == lax.axis_size("depth") - 1).astype(jnp.int32),
            slab % 2,
        ]
    ).astype(jnp.int32)
    state, message = load_nodes(gd, gv, cd, cv, den, hist, cells, flags)
    rx = ring(message, "slab", -1)
    memory, sums, moduli = memory_part(gm, cm, lam, mu, dm)
    message = depth_message(state, rx, moduli)
    ry = ring(message, "depth", -1)
    part = filter_part(hist, cells, filters, rx, message)[None]
    u, v, inv, force, strain, first, second = first_step(state, rx, ry, flags, moduli, sums)
    strains, samples = [strain], []
    for step in range(1, STEPS + 1):
        yb = swap(second, "depth", 1)
        ya = swap(first, "depth", 0)
        edge, first, second = fold_depth(force, ya, yb, flags)
        xb = swap(second, "slab", 1)
        xa = swap(first, "slab", 0)
        if step == 1:
            reach = 1
            while reach < lax.axis_size("depth"):
                part = join(part, ring(part, "depth", -reach), edge)
                reach *= 2
            surface = surface_part(part, flags[1:2])
        if step < STEPS:
            sums = next_sums(step, kept, memory, strains)
            u, v, force, strain, first, second, sample = next_step(
                step, u, v, inv, force, edge, xa, xb, flags, surface, moduli, sums, samples
            )
            strains.append(strain)
            samples.append(sample)
        else:
            gm_out, cm_out = final_memory(kept, memory, strains, gm.shape)
            gd_out, gv_out, cd_out, cv_out = finish(
                u, v, inv, force, edge, xa, xb, flags, surface, samples, gd.shape
            )
    return gd_out, gv_out, gm_out, cd_out, cv_out, cm_out


def solution(mesh):
    nodes = P(None, "slab", "depth", None)
    memory = P(None, None, None, None, None, "slab", "depth", None)
    points = P(None, None, None, "slab", "depth", None)
    return jax.shard_map(
        body,
        mesh=mesh,
        in_specs=(
            nodes,
            nodes,
            memory,
            nodes,
            nodes,
            memory,
            points,
            points,
            points,
            P(),
            P("slab", "depth", None),
            P(None, "slab", "depth"),
            P("slab", "depth"),
            P(),
        ),
        out_specs=(nodes, nodes, memory, nodes, nodes, memory),
        check_vma=False,
    )
```

```python
import functools

import jax
import jax.numpy as jnp
import numpy as np
from jax import lax
from jax.experimental import pallas as pl
from jax.experimental.pallas import tpu as pltpu
from jax.sharding import PartitionSpec as P

STEPS = 4
TAPS = 64
GLL = 5
SLS = 3
COMP = 5
LANES = 128
TILE = 8
COLS = GLL * GLL
ROWS = COLS * TILE
time_step = 0.04
f32 = jnp.float32
bf16 = jnp.bfloat16

VM = pl.BlockSpec(memory_space=pltpu.VMEM)
SM = pl.BlockSpec(memory_space=pltpu.SMEM)
HB = pl.BlockSpec(memory_space=pltpu.HBM)


def gll_tables():
    points = np.array([-1.0, -np.sqrt(3.0 / 7.0), 0.0, np.sqrt(3.0 / 7.0), 1.0])
    weights = np.array([0.1, 49.0 / 90.0, 32.0 / 45.0, 49.0 / 90.0, 0.1])
    number = points.shape[0]
    products = np.array(
        [
            np.prod([points[t] - points[o] for o in range(number) if o != t])
            for t in range(number)
        ]
    )
    derivative = np.zeros((number, number))
    for t in range(number):
        for s in range(number):
            if t == s:
                derivative[t, s] = np.sum(
                    [1.0 / (points[t] - points[o]) for o in range(number) if o != t]
                )
            else:
                derivative[t, s] = products[t] / products[s] / (points[t] - points[s])
    return derivative, weights


DMAT, WEIGHTS = gll_tables()
NODE_W = [0.2, 49.0 / 90.0, 32.0 / 45.0, 49.0 / 90.0, 0.2]


def tile_rows(a, b):
    return pl.ds((a * GLL + b) * TILE, TILE)


def at_tile(a, b):
    return pl.ds(pl.multiple_of((a * GLL + b) * TILE, TILE), TILE)


def at_nodes(a, b):
    return pl.ds(pl.multiple_of((a * GLL + b) * TILE, TILE), 4)


def row_index():
    return lax.broadcasted_iota(jnp.int32, (TILE, LANES), 0)


def row_vector(values):
    rows = row_index()
    out = jnp.zeros((TILE, LANES), f32)
    for index, value in enumerate(values):
        out = jnp.where(rows == index, f32(value), out)
    return out


def contract(x, t):
    e0, e1, o0, o1 = x[0] + x[4], x[1] + x[3], x[0] - x[4], x[1] - x[3]

    def odd(p):
        return float((t[p, 0] - t[p, 4]) / 2) * o0 + float((t[p, 1] - t[p, 3]) / 2) * o1

    def even(p):
        return (
            float((t[p, 0] + t[p, 4]) / 2) * e0
            + float((t[p, 1] + t[p, 3]) / 2) * e1
            + float(t[p, 2]) * x[2]
        )

    s0, s1, s2, a0, a1 = odd(0), odd(1), odd(2), even(0), even(1)
    return [s0 + a0, s1 + a1, s2, s1 - a1, s0 - a0]


def permutation(transposed):
    size = 4 * LANES
    first = lax.broadcasted_iota(jnp.int32, (size, size), 0)
    second = lax.broadcasted_iota(jnp.int32, (size, size), 1)
    node, place = (second, first) if transposed else (first, second)
    hit = node == 4 * (place & (LANES - 1)) + (place >> 7)
    return jnp.where(hit, f32(1), f32(0)).astype(bf16)


def exact_dot(x, p):
    high = x.astype(bf16)
    rest = x - high.astype(f32)
    mid = rest.astype(bf16)
    low = (rest - mid.astype(f32)).astype(bf16)
    dot = functools.partial(jnp.dot, preferred_element_type=f32)
    return (dot(low, p) + dot(mid, p)) + dot(high, p)


def call(kernel, outs, in_specs, out_specs=None, scratch=(), aliases=None, name=None, limit=10):
    run = pl.pallas_call(
        kernel,
        out_shape=tuple(
            pltpu.VMEM(o, f32) if out_specs is None else jax.ShapeDtypeStruct(o, f32) for o in outs
        ),
        in_specs=in_specs,
        out_specs=out_specs if out_specs is not None else tuple(VM for _ in outs),
        scratch_shapes=list(scratch),
        input_output_aliases=aliases or {},
        name=name,
        compiler_params=pltpu.CompilerParams(vmem_limit_bytes=limit << 20),
    )

    def placed(*operands):
        spaces = {id(VM): pltpu.VMEM, id(HB): pltpu.HBM}
        return run(
            *(
                pltpu.with_memory_space_constraint(o, spaces[id(s)]) if id(s) in spaces else o
                for o, s in zip(operands, in_specs)
            )
        )

    return placed


def load_kernel(gd, gv, cd, cv, den, hist, cells, flags, state, message, x, hrow, crow, sem):
    copies = []
    for base, array in ((0, gd), (3, gv), (6, cd), (9, cv)):
        for a in range(4):
            copies.append(
                pltpu.make_async_copy(
                    array.at[:, a],
                    x.at[pl.ds(base, 3), a // 2, pl.ds(4 * (a % 2), 4), :],
                    sem.at[len(copies)],
                )
            )
    for a in range(4):
        copies.append(
            pltpu.make_async_copy(
                den.at[a], x.at[12, a // 2, pl.ds(4 * (a % 2), 4), :], sem.at[len(copies)]
            )
        )
    copies.append(pltpu.make_async_copy(hist.at[:, 0], hrow, sem.at[len(copies)]))
    copies.append(pltpu.make_async_copy(cells, crow, sem.at[len(copies)]))
    for c in copies:
        c.start()
    p = permutation(False)
    for c in copies:
        c.wait()
    y = exact_dot(x[...].reshape(26 * TILE, 4 * LANES), p)
    for m in range(13):
        for a in range(4):
            for c in range(4):
                row = (2 * m + a // 2) * TILE + 4 * (a % 2)
                state[m, pl.ds(a * 40 + c, 4, stride=TILE), :] = y[
                    row : row + 4, c * LANES : (c + 1) * LANES
                ]
    for m in range(13):
        for b in range(4):
            message[m * 4 + b] = state[m, pl.ds(b * TILE, 4), :]
    for k in range(16):
        message[52 + k] = hrow[pl.ds(4 * k, 4), :]
    message[68] = jnp.broadcast_to(crow[0:1, :].astype(f32), (4, LANES))


def load_nodes(gd, gv, cd, cv, den, hist, cells, flags):
    return call(
        load_kernel,
        [(13, ROWS, LANES), (69, 4, LANES)],
        [HB] * 7 + [SM],
        scratch=[
            pltpu.VMEM((13, 2, TILE, 4 * LANES), f32),
            pltpu.VMEM((TAPS, LANES), f32),
            pltpu.VMEM((4, LANES), jnp.int32),
            pltpu.SemaphoreType.DMA((22,)),
        ],
        name="load_nodes",
    )(gd, gv, cd, cv, den, hist, cells, flags)


def depth_kernel(state, received, after, message):
    for m in range(13):
        for a in range(4):
            message[m * 5 + a] = state[m, pl.ds(a * 40, 4), :]
        message[m * 5 + 4] = received[m * 4]


def depth_message(state, received, after):
    return call(depth_kernel, [(65, 4, LANES)], [VM] * 3, name="depth_message")(
        state, received, after
    )[0]


def filter_kernel(hist_in, cells_in, filters_in, received, after, out, window, hist, cells, filters, sem):
    copies = []
    for source, target in ((hist_in, hist), (cells_in, cells), (filters_in, filters)):
        copies.append(pltpu.make_async_copy(source, target, sem.at[len(copies)]))
        copies[-1].start()
    for c in copies:
        c.wait()
    count = filters.shape[1]
    table = filters[...]
    high = table.astype(bf16)
    rest = table - high.astype(f32)
    mid = rest.astype(bf16)
    low = (rest - mid.astype(f32)).astype(bf16)
    stack = jnp.concatenate([high, mid, low], axis=0)
    ids = lax.broadcasted_iota(jnp.int32, (count, LANES), 0)
    for k in range(16):
        window[pl.ds(4 * k, 4), :] = received[52 + k]
    for x in range(5):
        if x < 4:
            cell = cells[x : x + 1, :]
            past = hist[:, x, :]
        else:
            cell = received[68][0:1, :].astype(jnp.int32)
            past = window[...]
        one_hot = jnp.where(ids == cell, f32(1), f32(0)).astype(bf16)
        t3 = jnp.dot(stack, one_hot, preferred_element_type=f32)
        taps = (t3[2 * TAPS :] + t3[TAPS : 2 * TAPS]) + t3[:TAPS]
        for lag in range(STEPS):
            kept = TAPS - 1 - lag
            out[lag, pl.ds(x, 1), :] = jnp.sum(
                taps[:kept] * past[lag + 1 :], axis=0, keepdims=True
            )
            out[STEPS + lag, pl.ds(x, 1), :] = taps[TAPS - STEPS + lag : TAPS - STEPS + lag + 1]


def filter_part(hist, cells, filters, received, after):
    return call(
        filter_kernel,
        [(2 * STEPS, TILE, LANES)],
        [HB] * 3 + [VM] * 2,
        scratch=[
            pltpu.VMEM((TAPS, LANES), f32),
            pltpu.VMEM(hist.shape, f32),
            pltpu.VMEM(cells.shape, jnp.int32),
            pltpu.VMEM(filters.shape, f32),
            pltpu.SemaphoreType.DMA((3,)),
        ],
        name="filter_part",
    )(hist, cells, filters, received, after)[0]


def join_kernel(mine, other, after, out):
    half = out.shape[0] // 2
    out[pl.ds(0, half)] = mine[...]
    out[pl.ds(half, half)] = other[...]


def join(mine, other, after):
    return call(
        join_kernel, [(2 * mine.shape[0],) + mine.shape[1:]], [VM] * 3, name="join"
    )(mine, other, after)[0]


def surface_kernel(chunks, top, out, z):
    on_top = top[0]
    for k in range(2 * STEPS):
        for d in range(4):
            z[k, :, pl.ds(d * LANES, LANES)] = chunks[d, k]
    y = exact_dot(z[...].reshape(2 * STEPS * TILE, 4 * LANES), permutation(False))
    keep = on_top > 0
    y = jnp.where(keep, y, f32(0))
    for k in range(2 * STEPS):
        for c in range(4):
            out[k, pl.ds(c, TILE, stride=TILE), :] = y[
                k * TILE : (k + 1) * TILE, c * LANES : (c + 1) * LANES
            ]


def surface_part(chunks, top):
    return call(
        surface_kernel,
        [(2 * STEPS, TILE * TILE, LANES)],
        [VM, SM],
        scratch=[pltpu.VMEM((2 * STEPS, TILE, 4 * LANES), f32)],
        name="surface_part",
    )(chunks, top)[0]


def memory_kernel(gm, cm, lam, mu, dm, memory, sums, moduli, sem):
    copies = []
    for f, array in enumerate((gm, cm)):
        for l in range(SLS):
            copies.append(
                pltpu.make_async_copy(
                    array.at[l, :, :, :, :, 0, 0, :],
                    memory.at[f, l, :, :, :, pl.ds(0, GLL), :],
                    sem.at[len(copies)],
                )
            )
    for index, array in enumerate((lam, mu, dm)):
        copies.append(
            pltpu.make_async_copy(
                array.at[:, :, :, 0, 0, :],
                moduli.at[index, :, :, pl.ds(0, GLL), :],
                sem.at[len(copies)],
            )
        )
    for c in copies:
        c.start()
    for c in copies:
        c.wait()
    wz = row_vector(WEIGHTS)
    for a in range(GLL):
        for b in range(GLL):
            w = wz * float(WEIGHTS[a] * WEIGHTS[b])
            shear = moduli[1, a, b] * w
            moduli[0, a, b] = moduli[0, a, b] * w
            moduli[1, a, b] = shear
            moduli[2, a, b] = moduli[2, a, b] * (2.0 * shear)

    def body(k, carry):
        for f in range(2):
            for a in range(GLL):
                for b in range(GLL):
                    w = wz * float(WEIGHTS[a] * WEIGHTS[b])
                    total = (memory[f, 0, k, a, b] + memory[f, 1, k, a, b]) + memory[f, 2, k, a, b]
                    sums[f, k, pl.ds((a * GLL + b) * TILE, TILE), :] = total * w
        return carry

    lax.fori_loop(0, COMP, body, 0)


def memory_part(gm, cm, lam, mu, dm):
    return call(
        memory_kernel,
        [
            (2, SLS, COMP, GLL, GLL, TILE, LANES),
            (2, COMP, ROWS, LANES),
            (3, GLL, GLL, TILE, LANES),
        ],
        [HB] * 5,
        scratch=[pltpu.SemaphoreType.DMA((9,))],
        name="memory_part",
    )(gm, cm, lam, mu, dm)


def sums_kernel(step, kept, memory, *refs):
    strains, sums = refs[:-1], refs[-1]
    k = [kept[l] for l in range(SLS)]

    def power(value, n):
        out = value
        for _ in range(n - 1):
            out = out * value
        return out

    grow = [power(k[l], step) for l in range(SLS)]
    past = []
    for s in range(step):
        n = step - 1 - s
        total = None
        for l in range(SLS):
            term = (1.0 - k[l]) * power(k[l], n) if n else 1.0 - k[l]
            total = term if total is None else total + term
        past.append(total)
    wz = row_vector(WEIGHTS)
    scaled = [[wz * grow[l] for l in range(SLS)]][0]

    def body(j, carry):
        for f in range(2):
            for a in range(GLL):
                for b in range(GLL):
                    here = pl.ds((a * GLL + b) * TILE, TILE)
                    w = float(WEIGHTS[a] * WEIGHTS[b])
                    total = scaled[0] * memory[f, 0, j, a, b]
                    for l in range(1, SLS):
                        total = total + scaled[l] * memory[f, l, j, a, b]
                    total = total * w
                    for s in range(step):
                        total = total + past[s] * strains[s][f, j, here, :]
                    sums[f, j, here, :] = total
        return carry

    lax.fori_loop(0, COMP, body, 0)


def next_sums(step, kept, memory, strains):
    return call(
        functools.partial(sums_kernel, step),
        [(2, COMP, ROWS, LANES)],
        [SM] + [VM] * (1 + len(strains)),
        name=f"sums_{step}",
    )(kept, memory, *strains)[0]


def final_memory_kernel(kept, memory, q0, q1, q2, q3, gout, cout, out, sem):
    strains = (q0, q1, q2, q3)
    iz = row_vector([1.0 / w for w in WEIGHTS])
    coefficients = []
    for l in range(SLS):
        k = kept[l]
        k2 = k * k
        scale = iz * (1.0 - k)
        coefficients.append((k2 * k2, [scale * (k2 * k), scale * k2, scale * k, scale]))

    copies = []
    for f, target in enumerate((gout, cout)):

        def body(j, carry, f=f):
            for a in range(GLL):
                for b in range(GLL):
                    here = pl.ds((a * GLL + b) * TILE, TILE)
                    iw = float(1.0 / (WEIGHTS[a] * WEIGHTS[b]))
                    q = [s[f, j, here, :] * iw for s in strains]
                    for l in range(SLS):
                        decay, cs = coefficients[l]
                        out[f, l, j, a, b] = decay * memory[f, l, j, a, b] + (
                            (cs[0] * q[0] + cs[1] * q[1]) + (cs[2] * q[2] + cs[3] * q[3])
                        )
            return carry

        lax.fori_loop(0, COMP, body, 0)
        for l in range(SLS):
            copy = pltpu.make_async_copy(
                out.at[f, l, :, :, :, pl.ds(0, GLL), :],
                target.at[l, :, :, :, :, 0, 0, :],
                sem.at[len(copies)],
            )
            copy.start()
            copies.append(copy)
    for c in copies:
        c.wait()


def final_memory(kept, memory, strains, shape):
    return call(
        final_memory_kernel,
        [shape, shape],
        [SM] + [VM] * 5,
        out_specs=(HB, HB),
        scratch=[
            pltpu.VMEM((2, SLS, COMP, GLL, GLL, TILE, LANES), f32),
            pltpu.SemaphoreType.DMA((6,)),
        ],
        name="final_memory",
    )(kept, memory, *strains)


ALONG = ((0, 3, 4), (3, 1, 5), (4, 5, 2))


def stresses(f, u, moduli, sums, grad, stress, strain):
    dz = [row_vector(DMAT[:, q]) for q in range(GLL)]
    for i in range(3):
        for b in range(GLL):
            out = contract([u[f, i, tile_rows(a, b), :] for a in range(GLL)], DMAT)
            for a in range(GLL):
                grad[i, tile_rows(a, b), :] = out[a]
        for a in range(GLL):
            out = contract([u[f, i, tile_rows(a, b), :] for b in range(GLL)], DMAT)
            for b in range(GLL):
                grad[3 + i, tile_rows(a, b), :] = out[b]
    for a in range(GLL):
        for b in range(GLL):
            here = tile_rows(a, b)
            gz = []
            for i in range(3):
                total = None
                for q in range(GLL):
                    row = u[f, i, pl.ds((a * GLL + b) * TILE + q, TILE, stride=0), :]
                    total = dz[q] * row if total is None else total + dz[q] * row
                gz.append(total)
            gx = [grad[i, here, :] for i in range(3)]
            gy = [grad[3 + i, here, :] for i in range(3)]
            lam, mu, dm = moduli[0, a, b], moduli[1, a, b], moduli[2, a, b]
            s = [sums[f, j, here, :] for j in range(COMP)]
            exx, eyy, ezz = gx[0], gy[1], gz[2]
            hxy, hxz, hyz = gy[0] + gx[1], gz[0] + gx[2], gz[1] + gy[2]
            volume = exx + eyy + ezz
            third = volume * f32(1.0 / 3.0)
            mu2 = mu + mu
            pressure = lam * volume
            half = dm * f32(0.5)
            strain[f, 0, here, :] = dm * (exx - third)
            strain[f, 1, here, :] = dm * (eyy - third)
            strain[f, 2, here, :] = half * hxy
            strain[f, 3, here, :] = half * hxz
            strain[f, 4, here, :] = half * hyz
            stress[f, 0, here, :] = pressure + mu2 * exx - s[0]
            stress[f, 1, here, :] = pressure + mu2 * eyy - s[1]
            stress[f, 2, here, :] = pressure + mu2 * ezz + (s[0] + s[1])
            stress[f, 3, here, :] = mu * hxy - s[2]
            stress[f, 4, here, :] = mu * hxz - s[3]
            stress[f, 5, here, :] = mu * hyz - s[4]


def corner_forces(f, stress, corner):
    tz = [row_vector(DMAT[p, :]) for p in range(GLL)]
    rows = row_index()
    for i in range(3):
        for a in (0, 4):
            for b in (0, 4):
                total = None
                for p in range(GLL):
                    row = stress[
                        f, ALONG[2][i], pl.ds((a * GLL + b) * TILE + p, TILE, stride=0), :
                    ]
                    term = (
                        float(DMAT[p, a]) * stress[f, ALONG[0][i], tile_rows(p, b), :]
                        + float(DMAT[p, b]) * stress[f, ALONG[1][i], tile_rows(a, p), :]
                    ) + tz[p] * row
                    total = term if total is None else total + term
                carried = pltpu.roll(pltpu.roll(total, 1, 1), 4, 0)
                corner[f, i, (a // 4) * 2 + b // 4] = total + jnp.where(rows == 0, carried, f32(0))


def rest_forces(f, stress, grad, force):
    tz = [row_vector(DMAT[p, :]) for p in range(GLL)]
    rows = row_index()
    for i in range(3):
        for b in range(GLL):
            out = contract(
                [stress[f, ALONG[0][i], tile_rows(a, b), :] for a in range(GLL)], DMAT.T
            )
            for a in range(GLL):
                grad[i, tile_rows(a, b), :] = out[a]
    for i in range(3):
        for a in range(GLL):
            out = contract(
                [stress[f, ALONG[1][i], tile_rows(a, b), :] for b in range(GLL)], DMAT.T
            )
            for b in range(GLL):
                here = tile_rows(a, b)
                total = out[b] + grad[i, here, :]
                for p in range(GLL):
                    row = stress[
                        f, ALONG[2][i], pl.ds((a * GLL + b) * TILE + p, TILE, stride=0), :
                    ]
                    total = total + tz[p] * row
                carried = pltpu.roll(pltpu.roll(total, 1, 1), 4, 0)
                force[f, i, here, :] = total + jnp.where(rows == 0, carried, f32(0))


def corner_messages(f, parity, corner, first, second):
    par = parity[0]
    for i in range(3):
        for a in range(2):
            first[f, i, a] = corner[f, i, 2 * a + 1 - par, pl.ds(0, 4), :]
            second[f, i, a] = corner[f, i, 2 * a + par, pl.ds(0, 4), :]


def with_end_row(x, rows):
    return jnp.where(rows == 4, pltpu.roll(pltpu.roll(x, LANES - 1, 1), 4, 0), x)


def first_kernel(
    state, rx, ry, flags, moduli, sums, u, v, inv, stress, strain, corner, first, second, grad
):
    rows = row_index()
    top, bottom = flags[1] > 0, flags[2] > 0
    wz = row_vector(NODE_W)

    def node(m, a, b, tmp):
        if b == 4:
            if m == 12:
                return ry[m * 5 + a]
            return jnp.where(bottom, f32(0), ry[m * 5 + a])
        if a == 4:
            return rx[m * 4 + b]
        return state[m, pl.ds((a * GLL + b) * TILE, 4), :]

    for a in range(GLL):
        for b in range(GLL):
            here = pl.ds((a * GLL + b) * TILE, 4)
            inv[here, :] = node(12, a, b, None)
    for a in range(GLL):
        for b in range(GLL):
            here = tile_rows(a, b)
            wy = f32(NODE_W[b])
            if b == 0:
                wy = jnp.where(top, f32(0.1), wy)
            mass = inv[here, :] * (wz * (wy * f32(NODE_W[a])))
            value = f32(time_step) / mass
            if b == 4:
                value = jnp.where(bottom, f32(0), value)
            inv[here, :] = value
    for f in range(2):
        for i in range(3):
            for a in range(GLL):
                for b in range(GLL):
                    here = tile_rows(a, b)
                    four = pl.ds((a * GLL + b) * TILE, 4)
                    u[f, i, four, :] = node(6 * f + i, a, b, None)
                    v[f, i, four, :] = node(6 * f + 3 + i, a, b, None)
    for f in range(2):
        for i in range(3):
            for a in range(GLL):
                for b in range(GLL):
                    here = tile_rows(a, b)
                    u[f, i, here, :] = with_end_row(u[f, i, here, :], rows)

    def body(f, carry):
        stresses(f, u, moduli, sums, grad, stress, strain)
        corner_forces(f, stress, corner)
        corner_messages(f, flags, corner, first, second)
        return carry

    lax.fori_loop(0, 2, body, 0)


STATE = (2, 3, ROWS, LANES)
FACE = (2, 3, GLL, 4, LANES)
STRESS = (2, 6, ROWS, LANES)
CORNER = (2, 3, 4, TILE, LANES)
CORNER_FACE = (2, 3, 2, 4, LANES)
INNER_FACE = (2, 3, 3, 4, LANES)
FACES = pltpu.VMEM((3, 2, GLL * TILE, LANES), f32)
SIDES = pltpu.VMEM((3, 2, 3 * TILE, LANES), f32)
WORK = [pltpu.VMEM((6, ROWS, LANES), f32)]


def first_step(state, rx, ry, flags, moduli, sums):
    return call(
        first_kernel,
        [STATE, STATE, (ROWS, LANES), STRESS, (2, COMP, ROWS, LANES), CORNER, CORNER_FACE, CORNER_FACE],
        [VM, VM, VM, SM, VM, VM],
        scratch=WORK,
        name="step_0",
    )(state, rx, ry, flags, moduli, sums)


def advance(
    f, step, u_in, v_in, inv, force, corner, got, flags, surface, samples, u, v, sample_out, face, side
):
    xa, xb, ya, yb = got
    rows = row_index()
    pd, top, ps = flags[0], flags[1] > 0, flags[3]
    for i in range(3):
        for slot, part in ((1 - ps, xa), (ps, xb)):
            for b in range(GLL):
                if b in (0, 4):
                    own = corner[f, i, 2 * slot + b // 4, pl.ds(0, 4), :]
                else:
                    own = force[f, i, at_nodes(4 * slot, b), :]
                face[i, slot, pl.ds(b * TILE, 4), :] = own + part[f, i, b]
        for a in range(1, 4):
            here = pl.ds((a - 1) * TILE, 4)
            side[i, 1 - pd, here, :] = (
                force[f, i, at_nodes(a, 4 * (1 - pd)), :] + ya[f, i, a - 1]
            )
            other = jnp.where(top, f32(0), yb[f, i, a - 1])
            side[i, pd, here, :] = force[f, i, at_nodes(a, 4 * pd), :] + other
    for i in range(3):
        for a in range(GLL):
            for b in range(GLL):
                here = tile_rows(a, b)
                scale = inv[here, :]
                if a in (0, 4):
                    total = face[i, a // 4, pl.ds(b * TILE, TILE), :]
                elif b in (0, 4):
                    total = side[i, b // 4, pl.ds((a - 1) * TILE, TILE), :]
                else:
                    total = force[f, i, here, :]
                if f == 1 and i == 1 and b == 0:
                    eight = pl.ds(a * TILE, TILE)
                    forcing = surface[step, eight, :]
                    for s in range(step):
                        forcing = (
                            forcing + surface[2 * STEPS - 1 - step + s, eight, :] * samples[s][a]
                        )
                    forcing = forcing + surface[2 * STEPS - 1, eight, :] * sample_out[a]
                    total = total - forcing
                velocity = v_in[f, i, here, :] - scale * total
                v[f, i, here, :] = velocity
                value = u_in[f, i, here, :] + f32(time_step) * velocity
                value = with_end_row(value, rows)
                u[f, i, here, :] = value
                if f == 0 and i == 1 and b == 0:
                    sample_out[a] = value


def step_kernel(
    step, u_in, v_in, inv, force, corner_in, xa, xb, ya, yb, flags, surface, moduli, sums, *refs
):
    samples, refs = refs[: step - 1], refs[step - 1 :]
    u, v, stress, strain, corner, first, second, sample_out, grad, face, side = refs
    got = (xa, xb, ya, yb)
    for f in range(2):
        advance(
            f, step - 1, u_in, v_in, inv, force, corner_in, got, flags, surface, samples, u, v,
            sample_out, face, side,
        )

    def body(f, carry):
        stresses(f, u, moduli, sums, grad, stress, strain)
        corner_forces(f, stress, corner)
        corner_messages(f, flags, corner, first, second)
        return carry

    lax.fori_loop(0, 2, body, 0)


def next_step(step, u, v, inv, force, corner, got, flags, surface, moduli, sums, samples):
    return call(
        functools.partial(step_kernel, step),
        [
            STATE,
            STATE,
            STRESS,
            (2, COMP, ROWS, LANES),
            CORNER,
            CORNER_FACE,
            CORNER_FACE,
            (GLL, TILE, LANES),
        ],
        [VM] * 9 + [SM] + [VM] * (3 + len(samples)),
        scratch=WORK + [FACES, SIDES],
        name=f"step_{step}",
    )(u, v, inv, force, corner, *got, flags, surface, moduli, sums, *samples)


def rest_kernel(stress, force, grad):
    def body(f, carry):
        rest_forces(f, stress, grad, force)
        return carry

    lax.fori_loop(0, 2, body, 0)


def rest_of_forces(stress):
    return call(
        rest_kernel,
        [STATE],
        [VM],
        scratch=[pltpu.VMEM((3, ROWS, LANES), f32)],
        name="rest_of_forces",
    )(stress)[0]


def fold_kernel(corner_in, force, ya, yb, flags, corner, first, second, inner_first, inner_second):
    pd, ps, top = flags[0], flags[3], flags[1] > 0
    four = pl.ds(0, 4)
    for f in range(2):
        for i in range(3):
            for a in range(2):
                high, low = 2 * a + 1 - pd, 2 * a + pd
                corner[f, i, high, four, :] = corner_in[f, i, high, four, :] + ya[f, i, a]
                other = jnp.where(top, f32(0), yb[f, i, a])
                corner[f, i, low, four, :] = corner_in[f, i, low, four, :] + other
            for out, a in ((first, 1 - ps), (second, ps)):
                for b in range(GLL):
                    if b in (0, 4):
                        out[f, i, b] = corner[f, i, 2 * a + b // 4, four, :]
                    else:
                        out[f, i, b] = force[f, i, at_nodes(4 * a, b), :]
            for a in range(1, 4):
                inner_first[f, i, a - 1] = force[f, i, at_nodes(a, 4 * (1 - pd)), :]
                inner_second[f, i, a - 1] = force[f, i, at_nodes(a, 4 * pd), :]


def fold_depth(corner, force, ya, yb, flags):
    return call(
        fold_kernel,
        [CORNER, FACE, FACE, INNER_FACE, INNER_FACE],
        [VM] * 4 + [SM],
        name="fold_depth",
    )(corner, force, ya, yb, flags)


def finish_kernel(
    u_in, v_in, inv, force, corner, xa, xb, ya, yb, flags, surface, s0, s1, s2, gd, gv, cd, cv,
    u, v, last, face, side, z, sem
):
    got = (xa, xb, ya, yb)
    for f in range(2):
        advance(
            f, STEPS - 1, u_in, v_in, inv, force, corner, got, flags, surface, (s0, s1, s2), u, v,
            last, face, side,
        )
    for f in range(2):
        for kind, array in enumerate((u, v)):
            for i in range(3):
                m = (f * 2 + kind) * 3 + i
                for a in range(4):
                    for c in range(4):
                        z[m, a // 2, pl.ds(4 * (a % 2), 4), pl.ds(c * LANES, LANES)] = array[
                            f, i, pl.ds(a * 40 + c, 4, stride=TILE), :
                        ]
    out = exact_dot(z[...].reshape(24 * TILE, 4 * LANES), permutation(True))
    z[...] = out.reshape(12, 2, TILE, 4 * LANES)
    copies = []
    for k, target in enumerate((gd, gv, cd, cv)):
        for a in range(4):
            copy = pltpu.make_async_copy(
                z.at[pl.ds(3 * k, 3), a // 2, pl.ds(4 * (a % 2), 4), :],
                target.at[:, a],
                sem.at[len(copies)],
            )
            copy.start()
            copies.append(copy)
    for c in copies:
        c.wait()


def finish(u, v, inv, force, corner, got, flags, surface, samples, shape):
    return call(
        finish_kernel,
        [shape] * 4,
        [VM] * 9 + [SM] + [VM] * 4,
        out_specs=(HB,) * 4,
        scratch=[
            pltpu.VMEM(STATE, f32),
            pltpu.VMEM(STATE, f32),
            pltpu.VMEM((GLL, TILE, LANES), f32),
            FACES,
            SIDES,
            pltpu.VMEM((12, 2, TILE, 4 * LANES), f32),
            pltpu.SemaphoreType.DMA((16,)),
        ],
        name="finish",
    )(u, v, inv, force, corner, *got, flags, surface, *samples)


def ring(value, axis, steps):
    count = lax.axis_size(axis)
    return lax.ppermute(value, axis, [(s, (s + steps) % count) for s in range(count)])


def swap(value, axis, offset):
    count = lax.axis_size(axis)
    pairs = []
    for s in range(offset, count + offset, 2):
        pairs += [(s % count, (s + 1) % count), ((s + 1) % count, s % count)]
    return lax.ppermute(value, axis, pairs)


def body(gd, gv, gm, cd, cv, cm, lam, mu, dm, kept, den, hist, cells, filters):
    filters = filters.T
    slab, depth = lax.axis_index("slab"), lax.axis_index("depth")
    flags = jnp.stack(
        [
            depth % 2,
            (depth == 0).astype(jnp.int32),
            (depth == lax.axis_size("depth") - 1).astype(jnp.int32),
            slab % 2,
        ]
    ).astype(jnp.int32)
    state, message = load_nodes(gd, gv, cd, cv, den, hist, cells, flags)
    rx = ring(message, "slab", -1)
    memory, sums, moduli = memory_part(gm, cm, lam, mu, dm)
    message = depth_message(state, rx, moduli)
    ry = ring(message, "depth", -1)
    part = filter_part(hist, cells, filters, rx, message)[None]
    u, v, inv, stress, strain, corner, first, second = first_step(
        state, rx, ry, flags, moduli, sums
    )
    strains, samples = [strain], []
    for step in range(1, STEPS + 1):
        yb = swap(second, "depth", 1)
        ya = swap(first, "depth", 0)
        force = rest_of_forces(stress)
        corner, first, second, inner_first, inner_second = fold_depth(corner, force, ya, yb, flags)
        xb = swap(second, "slab", 1)
        yb = swap(inner_second, "depth", 1)
        ya = swap(inner_first, "depth", 0)
        xa = swap(first, "slab", 0)
        got = (xa, xb, ya, yb)
        if step == 1:
            reach = 1
            while reach < lax.axis_size("depth"):
                part = join(part, ring(part, "depth", -reach), corner)
                reach *= 2
            surface = surface_part(part, flags[1:2])
        if step < STEPS:
            sums = next_sums(step, kept, memory, strains)
            u, v, stress, strain, corner, first, second, sample = next_step(
                step, u, v, inv, force, corner, got, flags, surface, moduli, sums, samples
            )
            strains.append(strain)
            samples.append(sample)
        else:
            gm_out, cm_out = final_memory(kept, memory, strains, gm.shape)
            gd_out, gv_out, cd_out, cv_out = finish(
                u, v, inv, force, corner, got, flags, surface, samples, gd.shape
            )
    return gd_out, gv_out, gm_out, cd_out, cv_out, cm_out


def solution(mesh):
    nodes = P(None, "slab", "depth", None)
    memory = P(None, None, None, None, None, "slab", "depth", None)
    points = P(None, None, None, "slab", "depth", None)
    return jax.shard_map(
        body,
        mesh=mesh,
        in_specs=(
            nodes,
            nodes,
            memory,
            nodes,
            nodes,
            memory,
            points,
            points,
            points,
            P(),
            P("slab", "depth", None),
            P(None, "slab", "depth"),
            P("slab", "depth"),
            P(),
        ),
        out_specs=(nodes, nodes, memory, nodes, nodes, memory),
        check_vma=False,
    )
```

```python
import functools

import jax
import jax.numpy as jnp
import numpy as np
from jax import lax
from jax.experimental import pallas as pl
from jax.experimental.pallas import tpu as pltpu
from jax.sharding import PartitionSpec as P

STEPS = 4
TAPS = 64
GLL = 5
SLS = 3
COMP = 5
LANES = 128
TILE = 8
COLS = GLL * GLL
ROWS = COLS * TILE
time_step = 0.04
f32 = jnp.float32
bf16 = jnp.bfloat16

VM = pl.BlockSpec(memory_space=pltpu.VMEM)
SM = pl.BlockSpec(memory_space=pltpu.SMEM)
HB = pl.BlockSpec(memory_space=pltpu.HBM)


def gll_tables():
    points = np.array([-1.0, -np.sqrt(3.0 / 7.0), 0.0, np.sqrt(3.0 / 7.0), 1.0])
    weights = np.array([0.1, 49.0 / 90.0, 32.0 / 45.0, 49.0 / 90.0, 0.1])
    number = points.shape[0]
    products = np.array(
        [
            np.prod([points[t] - points[o] for o in range(number) if o != t])
            for t in range(number)
        ]
    )
    derivative = np.zeros((number, number))
    for t in range(number):
        for s in range(number):
            if t == s:
                derivative[t, s] = np.sum(
                    [1.0 / (points[t] - points[o]) for o in range(number) if o != t]
                )
            else:
                derivative[t, s] = products[t] / products[s] / (points[t] - points[s])
    return derivative, weights


DMAT, WEIGHTS = gll_tables()
NODE_W = [0.2, 49.0 / 90.0, 32.0 / 45.0, 49.0 / 90.0, 0.2]


def place():
    depth = lax.axis_index("depth")
    last = lax.axis_size("depth") - 1
    odd = (depth & 1, lax.axis_index("slab") & 1)
    return odd[0], depth == 0, depth == last, odd[1]


def tile_rows(a, b):
    return pl.ds((a * GLL + b) * TILE, TILE)


def at_tile(a, b):
    return pl.ds(pl.multiple_of((a * GLL + b) * TILE, TILE), TILE)


def at_nodes(a, b):
    return pl.ds(pl.multiple_of((a * GLL + b) * TILE, TILE), 4)


def row_index():
    return lax.broadcasted_iota(jnp.int32, (TILE, LANES), 0)


def row_vector(values):
    rows = row_index()
    out = jnp.zeros((TILE, LANES), f32)
    for index, value in enumerate(values):
        out = jnp.where(rows == index, f32(value), out)
    return out


def contract(x, t):
    e0, e1, o0, o1 = x[0] + x[4], x[1] + x[3], x[0] - x[4], x[1] - x[3]

    def odd(p):
        return float((t[p, 0] - t[p, 4]) / 2) * o0 + float((t[p, 1] - t[p, 3]) / 2) * o1

    def even(p):
        return (
            float((t[p, 0] + t[p, 4]) / 2) * e0
            + float((t[p, 1] + t[p, 3]) / 2) * e1
            + float(t[p, 2]) * x[2]
        )

    s0, s1, s2, a0, a1 = odd(0), odd(1), odd(2), even(0), even(1)
    return [s0 + a0, s1 + a1, s2, s1 - a1, s0 - a0]


def permutation(transposed):
    size = 4 * LANES
    first = lax.broadcasted_iota(jnp.int32, (size, size), 0)
    second = lax.broadcasted_iota(jnp.int32, (size, size), 1)
    node, place = (second, first) if transposed else (first, second)
    hit = node == 4 * (place & (LANES - 1)) + (place >> 7)
    return jnp.where(hit, f32(1), f32(0)).astype(bf16)


def exact_dot(x, p):
    high = x.astype(bf16)
    rest = x - high.astype(f32)
    mid = rest.astype(bf16)
    low = (rest - mid.astype(f32)).astype(bf16)
    dot = functools.partial(jnp.dot, preferred_element_type=f32)
    return (dot(low, p) + dot(mid, p)) + dot(high, p)


def call(kernel, outs, in_specs, out_specs=None, scratch=(), aliases=None, name=None, limit=10):
    run = pl.pallas_call(
        kernel,
        out_shape=tuple(
            pltpu.VMEM(o, f32) if out_specs is None else jax.ShapeDtypeStruct(o, f32) for o in outs
        ),
        in_specs=in_specs,
        out_specs=out_specs if out_specs is not None else tuple(VM for _ in outs),
        scratch_shapes=list(scratch),
        input_output_aliases=aliases or {},
        name=name,
        compiler_params=pltpu.CompilerParams(vmem_limit_bytes=limit << 20),
    )

    def placed(*operands):
        spaces = {id(VM): pltpu.VMEM, id(HB): pltpu.HBM}
        return run(
            *(
                pltpu.with_memory_space_constraint(o, spaces[id(s)]) if id(s) in spaces else o
                for o, s in zip(operands, in_specs)
            )
        )

    return placed


def load_kernel(gd, gv, cd, cv, den, hist, cells, state, message, x, hrow, crow, sem):
    copies = []
    for base, array in ((0, gd), (3, gv), (6, cd), (9, cv)):
        for a in range(4):
            copies.append(
                pltpu.make_async_copy(
                    array.at[:, a],
                    x.at[pl.ds(base, 3), a // 2, pl.ds(4 * (a % 2), 4), :],
                    sem.at[len(copies)],
                )
            )
    for a in range(4):
        copies.append(
            pltpu.make_async_copy(
                den.at[a], x.at[12, a // 2, pl.ds(4 * (a % 2), 4), :], sem.at[len(copies)]
            )
        )
    copies.append(pltpu.make_async_copy(hist.at[:, 0], hrow, sem.at[len(copies)]))
    copies.append(pltpu.make_async_copy(cells, crow, sem.at[len(copies)]))
    for c in copies:
        c.start()
    p = permutation(False)
    for c in copies:
        c.wait()
    y = exact_dot(x[...].reshape(26 * TILE, 4 * LANES), p)
    for m in range(13):
        for a in range(4):
            for c in range(4):
                row = (2 * m + a // 2) * TILE + 4 * (a % 2)
                state[m, pl.ds(a * 40 + c, 4, stride=TILE), :] = y[
                    row : row + 4, c * LANES : (c + 1) * LANES
                ]
    for m in range(13):
        for b in range(4):
            message[m * 4 + b] = state[m, pl.ds(b * TILE, 4), :]
    for k in range(16):
        message[52 + k] = hrow[pl.ds(4 * k, 4), :]
    message[68] = jnp.broadcast_to(crow[0:1, :].astype(f32), (4, LANES))


def load_nodes(gd, gv, cd, cv, den, hist, cells):
    return call(
        load_kernel,
        [(13, ROWS, LANES), (69, 4, LANES)],
        [HB] * 7,
        scratch=[
            pltpu.VMEM((13, 2, TILE, 4 * LANES), f32),
            pltpu.VMEM((TAPS, LANES), f32),
            pltpu.VMEM((4, LANES), jnp.int32),
            pltpu.SemaphoreType.DMA((22,)),
        ],
        name="load_nodes",
    )(gd, gv, cd, cv, den, hist, cells)


def depth_kernel(state, received, after, message):
    for m in range(13):
        for a in range(4):
            message[m * 5 + a] = state[m, pl.ds(a * 40, 4), :]
        message[m * 5 + 4] = received[m * 4]


def depth_message(state, received, after):
    return call(depth_kernel, [(65, 4, LANES)], [VM] * 3, name="depth_message")(
        state, received, after
    )[0]


def filter_kernel(hist_in, cells_in, filters_in, received, after, out, window, hist, cells, filters, sem):
    copies = []
    for source, target in ((hist_in, hist), (cells_in, cells), (filters_in, filters)):
        copies.append(pltpu.make_async_copy(source, target, sem.at[len(copies)]))
        copies[-1].start()
    for c in copies:
        c.wait()
    count = filters.shape[1]
    table = filters[...]
    high = table.astype(bf16)
    rest = table - high.astype(f32)
    mid = rest.astype(bf16)
    low = (rest - mid.astype(f32)).astype(bf16)
    stack = jnp.concatenate([high, mid, low], axis=0)
    ids = lax.broadcasted_iota(jnp.int32, (count, LANES), 0)
    for k in range(16):
        window[pl.ds(4 * k, 4), :] = received[52 + k]
    for x in range(5):
        if x < 4:
            cell = cells[x : x + 1, :]
            past = hist[:, x, :]
        else:
            cell = received[68][0:1, :].astype(jnp.int32)
            past = window[...]
        one_hot = jnp.where(ids == cell, f32(1), f32(0)).astype(bf16)
        t3 = jnp.dot(stack, one_hot, preferred_element_type=f32)
        taps = (t3[2 * TAPS :] + t3[TAPS : 2 * TAPS]) + t3[:TAPS]
        for lag in range(STEPS):
            kept = TAPS - 1 - lag
            out[lag, pl.ds(x, 1), :] = jnp.sum(
                taps[:kept] * past[lag + 1 :], axis=0, keepdims=True
            )
            out[STEPS + lag, pl.ds(x, 1), :] = taps[TAPS - STEPS + lag : TAPS - STEPS + lag + 1]


def filter_part(hist, cells, filters, received, after):
    return call(
        filter_kernel,
        [(2 * STEPS, TILE, LANES)],
        [HB] * 3 + [VM] * 2,
        scratch=[
            pltpu.VMEM((TAPS, LANES), f32),
            pltpu.VMEM(hist.shape, f32),
            pltpu.VMEM(cells.shape, jnp.int32),
            pltpu.VMEM(filters.shape, f32),
            pltpu.SemaphoreType.DMA((3,)),
        ],
        name="filter_part",
    )(hist, cells, filters, received, after)[0]


def join_kernel(mine, other, after, out):
    half = out.shape[0] // 2
    out[pl.ds(0, half)] = mine[...]
    out[pl.ds(half, half)] = other[...]


def join(mine, other, after):
    return call(
        join_kernel, [(2 * mine.shape[0],) + mine.shape[1:]], [VM] * 3, name="join"
    )(mine, other, after)[0]


def surface_kernel(chunks, out, z):
    for k in range(2 * STEPS):
        for d in range(4):
            z[k, :, pl.ds(d * LANES, LANES)] = chunks[d, k]
    y = exact_dot(z[...].reshape(2 * STEPS * TILE, 4 * LANES), permutation(False))
    y = jnp.where(place()[1], y, f32(0))
    for k in range(2 * STEPS):
        for c in range(4):
            out[k, pl.ds(c, TILE, stride=TILE), :] = y[
                k * TILE : (k + 1) * TILE, c * LANES : (c + 1) * LANES
            ]


def surface_part(chunks):
    return call(
        surface_kernel,
        [(2 * STEPS, TILE * TILE, LANES)],
        [VM],
        scratch=[pltpu.VMEM((2 * STEPS, TILE, 4 * LANES), f32)],
        name="surface_part",
    )(chunks)[0]


def memory_kernel(gm, cm, lam, mu, dm, memory, sums, moduli, sem):
    copies = []
    for f, array in enumerate((gm, cm)):
        for l in range(SLS):
            copies.append(
                pltpu.make_async_copy(
                    array.at[l, :, :, :, :, 0, 0, :],
                    memory.at[f, l, :, :, :, pl.ds(0, GLL), :],
                    sem.at[len(copies)],
                )
            )
    for index, array in enumerate((lam, mu, dm)):
        copies.append(
            pltpu.make_async_copy(
                array.at[:, :, :, 0, 0, :],
                moduli.at[index, :, :, pl.ds(0, GLL), :],
                sem.at[len(copies)],
            )
        )
    for c in copies:
        c.start()
    for c in copies:
        c.wait()
    wz = row_vector(WEIGHTS)
    for a in range(GLL):
        for b in range(GLL):
            w = wz * float(WEIGHTS[a] * WEIGHTS[b])
            shear = moduli[1, a, b] * w
            moduli[0, a, b] = moduli[0, a, b] * w
            moduli[1, a, b] = shear
            moduli[2, a, b] = moduli[2, a, b] * (2.0 * shear)

    def body(k, carry):
        for f in range(2):
            for a in range(GLL):
                for b in range(GLL):
                    w = wz * float(WEIGHTS[a] * WEIGHTS[b])
                    total = (memory[f, 0, k, a, b] + memory[f, 1, k, a, b]) + memory[f, 2, k, a, b]
                    sums[f, k, pl.ds((a * GLL + b) * TILE, TILE), :] = total * w
        return carry

    lax.fori_loop(0, COMP, body, 0)


def memory_part(gm, cm, lam, mu, dm):
    return call(
        memory_kernel,
        [
            (2, SLS, COMP, GLL, GLL, TILE, LANES),
            (2, COMP, ROWS, LANES),
            (3, GLL, GLL, TILE, LANES),
        ],
        [HB] * 5,
        scratch=[pltpu.SemaphoreType.DMA((9,))],
        name="memory_part",
    )(gm, cm, lam, mu, dm)


def sums_kernel(step, kept, memory, *refs):
    strains, sums = refs[:-1], refs[-1]
    k = [kept[l] for l in range(SLS)]

    def power(value, n):
        out = value
        for _ in range(n - 1):
            out = out * value
        return out

    grow = [power(k[l], step) for l in range(SLS)]
    past = []
    for s in range(step):
        n = step - 1 - s
        total = None
        for l in range(SLS):
            term = (1.0 - k[l]) * power(k[l], n) if n else 1.0 - k[l]
            total = term if total is None else total + term
        past.append(total)
    wz = row_vector(WEIGHTS)
    scaled = [[wz * grow[l] for l in range(SLS)]][0]

    def body(j, carry):
        for f in range(2):
            for a in range(GLL):
                for b in range(GLL):
                    here = pl.ds((a * GLL + b) * TILE, TILE)
                    w = float(WEIGHTS[a] * WEIGHTS[b])
                    total = scaled[0] * memory[f, 0, j, a, b]
                    for l in range(1, SLS):
                        total = total + scaled[l] * memory[f, l, j, a, b]
                    total = total * w
                    for s in range(step):
                        total = total + past[s] * strains[s][f, j, here, :]
                    sums[f, j, here, :] = total
        return carry

    lax.fori_loop(0, COMP, body, 0)


def next_sums(step, kept, memory, strains):
    return call(
        functools.partial(sums_kernel, step),
        [(2, COMP, ROWS, LANES)],
        [SM] + [VM] * (1 + len(strains)),
        name=f"sums_{step}",
    )(kept, memory, *strains)[0]


def final_memory_kernel(kept, memory, q0, q1, q2, q3, gout, cout, out, sem):
    strains = (q0, q1, q2, q3)
    iz = row_vector([1.0 / w for w in WEIGHTS])
    coefficients = []
    for l in range(SLS):
        k = kept[l]
        k2 = k * k
        scale = iz * (1.0 - k)
        coefficients.append((k2 * k2, [scale * (k2 * k), scale * k2, scale * k, scale]))

    copies = []
    for f, target in enumerate((gout, cout)):

        def body(j, carry, f=f):
            for a in range(GLL):
                for b in range(GLL):
                    here = pl.ds((a * GLL + b) * TILE, TILE)
                    iw = float(1.0 / (WEIGHTS[a] * WEIGHTS[b]))
                    q = [s[f, j, here, :] * iw for s in strains]
                    for l in range(SLS):
                        decay, cs = coefficients[l]
                        out[f, l, j, a, b] = decay * memory[f, l, j, a, b] + (
                            (cs[0] * q[0] + cs[1] * q[1]) + (cs[2] * q[2] + cs[3] * q[3])
                        )
            return carry

        lax.fori_loop(0, COMP, body, 0)
        for l in range(SLS):
            copy = pltpu.make_async_copy(
                out.at[f, l, :, :, :, pl.ds(0, GLL), :],
                target.at[l, :, :, :, :, 0, 0, :],
                sem.at[len(copies)],
            )
            copy.start()
            copies.append(copy)
    for c in copies:
        c.wait()


def final_memory(kept, memory, strains, shape):
    return call(
        final_memory_kernel,
        [shape, shape],
        [SM] + [VM] * 5,
        out_specs=(HB, HB),
        scratch=[
            pltpu.VMEM((2, SLS, COMP, GLL, GLL, TILE, LANES), f32),
            pltpu.SemaphoreType.DMA((6,)),
        ],
        name="final_memory",
    )(kept, memory, *strains)


ALONG = ((0, 3, 4), (3, 1, 5), (4, 5, 2))


def stresses(f, u, moduli, sums, grad, stress, strain):
    dz = [row_vector(DMAT[:, q]) for q in range(GLL)]
    for i in range(3):
        for b in range(GLL):
            out = contract([u[f, i, tile_rows(a, b), :] for a in range(GLL)], DMAT)
            for a in range(GLL):
                grad[i, tile_rows(a, b), :] = out[a]
        for a in range(GLL):
            out = contract([u[f, i, tile_rows(a, b), :] for b in range(GLL)], DMAT)
            for b in range(GLL):
                grad[3 + i, tile_rows(a, b), :] = out[b]
    for a in range(GLL):
        for b in range(GLL):
            here = tile_rows(a, b)
            gz = []
            for i in range(3):
                total = None
                for q in range(GLL):
                    row = u[f, i, pl.ds((a * GLL + b) * TILE + q, TILE, stride=0), :]
                    total = dz[q] * row if total is None else total + dz[q] * row
                gz.append(total)
            gx = [grad[i, here, :] for i in range(3)]
            gy = [grad[3 + i, here, :] for i in range(3)]
            lam, mu, dm = moduli[0, a, b], moduli[1, a, b], moduli[2, a, b]
            s = [sums[f, j, here, :] for j in range(COMP)]
            exx, eyy, ezz = gx[0], gy[1], gz[2]
            hxy, hxz, hyz = gy[0] + gx[1], gz[0] + gx[2], gz[1] + gy[2]
            volume = exx + eyy + ezz
            third = volume * f32(1.0 / 3.0)
            mu2 = mu + mu
            pressure = lam * volume
            half = dm * f32(0.5)
            strain[f, 0, here, :] = dm * (exx - third)
            strain[f, 1, here, :] = dm * (eyy - third)
            strain[f, 2, here, :] = half * hxy
            strain[f, 3, here, :] = half * hxz
            strain[f, 4, here, :] = half * hyz
            stress[f, 0, here, :] = pressure + mu2 * exx - s[0]
            stress[f, 1, here, :] = pressure + mu2 * eyy - s[1]
            stress[f, 2, here, :] = pressure + mu2 * ezz + (s[0] + s[1])
            stress[f, 3, here, :] = mu * hxy - s[2]
            stress[f, 4, here, :] = mu * hxz - s[3]
            stress[f, 5, here, :] = mu * hyz - s[4]


def corner_forces(f, stress, corner):
    tz = [row_vector(DMAT[p, :]) for p in range(GLL)]
    rows = row_index()
    for i in range(3):
        for a in (0, 4):
            for b in (0, 4):
                total = None
                for p in range(GLL):
                    row = stress[
                        f, ALONG[2][i], pl.ds((a * GLL + b) * TILE + p, TILE, stride=0), :
                    ]
                    term = (
                        float(DMAT[p, a]) * stress[f, ALONG[0][i], tile_rows(p, b), :]
                        + float(DMAT[p, b]) * stress[f, ALONG[1][i], tile_rows(a, p), :]
                    ) + tz[p] * row
                    total = term if total is None else total + term
                carried = pltpu.roll(pltpu.roll(total, 1, 1), 4, 0)
                corner[f, i, (a // 4) * 2 + b // 4] = total + jnp.where(rows == 0, carried, f32(0))


def rest_forces(f, stress, grad, force):
    tz = [row_vector(DMAT[p, :]) for p in range(GLL)]
    rows = row_index()
    for i in range(3):
        for b in range(GLL):
            out = contract(
                [stress[f, ALONG[0][i], tile_rows(a, b), :] for a in range(GLL)], DMAT.T
            )
            for a in range(GLL):
                grad[i, tile_rows(a, b), :] = out[a]
    for i in range(3):
        for a in range(GLL):
            out = contract(
                [stress[f, ALONG[1][i], tile_rows(a, b), :] for b in range(GLL)], DMAT.T
            )
            for b in range(GLL):
                here = tile_rows(a, b)
                total = out[b] + grad[i, here, :]
                for p in range(GLL):
                    row = stress[
                        f, ALONG[2][i], pl.ds((a * GLL + b) * TILE + p, TILE, stride=0), :
                    ]
                    total = total + tz[p] * row
                carried = pltpu.roll(pltpu.roll(total, 1, 1), 4, 0)
                force[f, i, here, :] = total + jnp.where(rows == 0, carried, f32(0))


def corner_messages(f, corner, first, second):
    par = place()[0]
    for i in range(3):
        for a in range(2):
            first[f, i, a] = corner[f, i, 2 * a + 1 - par, pl.ds(0, 4), :]
            second[f, i, a] = corner[f, i, 2 * a + par, pl.ds(0, 4), :]


def with_end_row(x, rows):
    return jnp.where(rows == 4, pltpu.roll(pltpu.roll(x, LANES - 1, 1), 4, 0), x)


def first_kernel(
    state, rx, ry, moduli, sums, u, v, inv, stress, strain, corner, first, second, grad
):
    rows = row_index()
    _, top, bottom, _ = place()
    wz = row_vector(NODE_W)

    def node(m, a, b, tmp):
        if b == 4:
            if m == 12:
                return ry[m * 5 + a]
            return jnp.where(bottom, f32(0), ry[m * 5 + a])
        if a == 4:
            return rx[m * 4 + b]
        return state[m, pl.ds((a * GLL + b) * TILE, 4), :]

    for a in range(GLL):
        for b in range(GLL):
            here = pl.ds((a * GLL + b) * TILE, 4)
            inv[here, :] = node(12, a, b, None)
    for a in range(GLL):
        for b in range(GLL):
            here = tile_rows(a, b)
            wy = f32(NODE_W[b])
            if b == 0:
                wy = jnp.where(top, f32(0.1), wy)
            mass = inv[here, :] * (wz * (wy * f32(NODE_W[a])))
            value = f32(time_step) / mass
            if b == 4:
                value = jnp.where(bottom, f32(0), value)
            inv[here, :] = value
    for f in range(2):
        for i in range(3):
            for a in range(GLL):
                for b in range(GLL):
                    here = tile_rows(a, b)
                    four = pl.ds((a * GLL + b) * TILE, 4)
                    u[f, i, four, :] = node(6 * f + i, a, b, None)
                    v[f, i, four, :] = node(6 * f + 3 + i, a, b, None)
    for f in range(2):
        for i in range(3):
            for a in range(GLL):
                for b in range(GLL):
                    here = tile_rows(a, b)
                    u[f, i, here, :] = with_end_row(u[f, i, here, :], rows)

    def body(f, carry):
        stresses(f, u, moduli, sums, grad, stress, strain)
        corner_forces(f, stress, corner)
        corner_messages(f, corner, first, second)
        return carry

    lax.fori_loop(0, 2, body, 0)


STATE = (2, 3, ROWS, LANES)
FACE = (2, 3, GLL, 4, LANES)
STRESS = (2, 6, ROWS, LANES)
CORNER = (2, 3, 4, TILE, LANES)
CORNER_FACE = (2, 3, 2, 4, LANES)
INNER_FACE = (2, 3, 3, 4, LANES)
FACES = pltpu.VMEM((3, 2, GLL * TILE, LANES), f32)
SIDES = pltpu.VMEM((3, 2, 3 * TILE, LANES), f32)
WORK = [pltpu.VMEM((6, ROWS, LANES), f32)]


def first_step(state, rx, ry, moduli, sums):
    return call(
        first_kernel,
        [STATE, STATE, (ROWS, LANES), STRESS, (2, COMP, ROWS, LANES), CORNER, CORNER_FACE, CORNER_FACE],
        [VM] * 5,
        scratch=WORK,
        name="step_0",
    )(state, rx, ry, moduli, sums)


def advance(
    f, step, u_in, v_in, inv, force, corner, got, surface, samples, u, v, sample_out, face, side
):
    xa, xb, ya, yb = got
    rows = row_index()
    pd, top, _, ps = place()
    for i in range(3):
        for slot, part in ((1 - ps, xa), (ps, xb)):
            for b in range(GLL):
                if b in (0, 4):
                    own = corner[f, i, 2 * slot + b // 4, pl.ds(0, 4), :]
                else:
                    own = force[f, i, at_nodes(4 * slot, b), :]
                face[i, slot, pl.ds(b * TILE, 4), :] = own + part[f, i, b]
        for a in range(1, 4):
            here = pl.ds((a - 1) * TILE, 4)
            side[i, 1 - pd, here, :] = (
                force[f, i, at_nodes(a, 4 * (1 - pd)), :] + ya[f, i, a - 1]
            )
            other = jnp.where(top, f32(0), yb[f, i, a - 1])
            side[i, pd, here, :] = force[f, i, at_nodes(a, 4 * pd), :] + other
    for i in range(3):
        for a in range(GLL):
            for b in range(GLL):
                here = tile_rows(a, b)
                scale = inv[here, :]
                if a in (0, 4):
                    total = face[i, a // 4, pl.ds(b * TILE, TILE), :]
                elif b in (0, 4):
                    total = side[i, b // 4, pl.ds((a - 1) * TILE, TILE), :]
                else:
                    total = force[f, i, here, :]
                if f == 1 and i == 1 and b == 0:
                    eight = pl.ds(a * TILE, TILE)
                    forcing = surface[step, eight, :]
                    for s in range(step):
                        forcing = (
                            forcing + surface[2 * STEPS - 1 - step + s, eight, :] * samples[s][a]
                        )
                    forcing = forcing + surface[2 * STEPS - 1, eight, :] * sample_out[a]
                    total = total - forcing
                velocity = v_in[f, i, here, :] - scale * total
                v[f, i, here, :] = velocity
                value = u_in[f, i, here, :] + f32(time_step) * velocity
                value = with_end_row(value, rows)
                u[f, i, here, :] = value
                if f == 0 and i == 1 and b == 0:
                    sample_out[a] = value


def step_kernel(
    step, u_in, v_in, inv, force, corner_in, xa, xb, ya, yb, surface, moduli, sums, *refs
):
    samples, refs = refs[: step - 1], refs[step - 1 :]
    u, v, stress, strain, corner, first, second, sample_out, grad, face, side = refs
    got = (xa, xb, ya, yb)
    for f in range(2):
        advance(
            f, step - 1, u_in, v_in, inv, force, corner_in, got, surface, samples, u, v,
            sample_out, face, side,
        )

    def body(f, carry):
        stresses(f, u, moduli, sums, grad, stress, strain)
        corner_forces(f, stress, corner)
        corner_messages(f, corner, first, second)
        return carry

    lax.fori_loop(0, 2, body, 0)


def next_step(step, u, v, inv, force, corner, got, surface, moduli, sums, samples):
    return call(
        functools.partial(step_kernel, step),
        [
            STATE,
            STATE,
            STRESS,
            (2, COMP, ROWS, LANES),
            CORNER,
            CORNER_FACE,
            CORNER_FACE,
            (GLL, TILE, LANES),
        ],
        [VM] * (12 + len(samples)),
        scratch=WORK + [FACES, SIDES],
        name=f"step_{step}",
    )(u, v, inv, force, corner, *got, surface, moduli, sums, *samples)


def rest_kernel(stress, force, grad):
    def body(f, carry):
        rest_forces(f, stress, grad, force)
        return carry

    lax.fori_loop(0, 2, body, 0)


def rest_of_forces(stress):
    return call(
        rest_kernel,
        [STATE],
        [VM],
        scratch=[pltpu.VMEM((3, ROWS, LANES), f32)],
        name="rest_of_forces",
    )(stress)[0]


def fold_kernel(corner_in, force, ya, yb, corner, first, second, inner_first, inner_second):
    pd, top, _, ps = place()
    four = pl.ds(0, 4)
    for f in range(2):
        for i in range(3):
            for a in range(2):
                high, low = 2 * a + 1 - pd, 2 * a + pd
                corner[f, i, high, four, :] = corner_in[f, i, high, four, :] + ya[f, i, a]
                other = jnp.where(top, f32(0), yb[f, i, a])
                corner[f, i, low, four, :] = corner_in[f, i, low, four, :] + other
            for out, a in ((first, 1 - ps), (second, ps)):
                for b in range(GLL):
                    if b in (0, 4):
                        out[f, i, b] = corner[f, i, 2 * a + b // 4, four, :]
                    else:
                        out[f, i, b] = force[f, i, at_nodes(4 * a, b), :]
            for a in range(1, 4):
                inner_first[f, i, a - 1] = force[f, i, at_nodes(a, 4 * (1 - pd)), :]
                inner_second[f, i, a - 1] = force[f, i, at_nodes(a, 4 * pd), :]


def fold_depth(corner, force, ya, yb):
    return call(
        fold_kernel,
        [CORNER, FACE, FACE, INNER_FACE, INNER_FACE],
        [VM] * 4,
        name="fold_depth",
    )(corner, force, ya, yb)


def finish_kernel(
    u_in, v_in, inv, force, corner, xa, xb, ya, yb, surface, s0, s1, s2, gd, gv, cd, cv,
    u, v, last, face, side, z, sem
):
    got = (xa, xb, ya, yb)
    for f in range(2):
        advance(
            f, STEPS - 1, u_in, v_in, inv, force, corner, got, surface, (s0, s1, s2), u, v,
            last, face, side,
        )
    for f in range(2):
        for kind, array in enumerate((u, v)):
            for i in range(3):
                m = (f * 2 + kind) * 3 + i
                for a in range(4):
                    for c in range(4):
                        z[m, a // 2, pl.ds(4 * (a % 2), 4), pl.ds(c * LANES, LANES)] = array[
                            f, i, pl.ds(a * 40 + c, 4, stride=TILE), :
                        ]
    out = exact_dot(z[...].reshape(24 * TILE, 4 * LANES), permutation(True))
    z[...] = out.reshape(12, 2, TILE, 4 * LANES)
    copies = []
    for k, target in enumerate((gd, gv, cd, cv)):
        for a in range(4):
            copy = pltpu.make_async_copy(
                z.at[pl.ds(3 * k, 3), a // 2, pl.ds(4 * (a % 2), 4), :],
                target.at[:, a],
                sem.at[len(copies)],
            )
            copy.start()
            copies.append(copy)
    for c in copies:
        c.wait()


def finish(u, v, inv, force, corner, got, surface, samples, shape):
    return call(
        finish_kernel,
        [shape] * 4,
        [VM] * 13,
        out_specs=(HB,) * 4,
        scratch=[
            pltpu.VMEM(STATE, f32),
            pltpu.VMEM(STATE, f32),
            pltpu.VMEM((GLL, TILE, LANES), f32),
            FACES,
            SIDES,
            pltpu.VMEM((12, 2, TILE, 4 * LANES), f32),
            pltpu.SemaphoreType.DMA((16,)),
        ],
        name="finish",
    )(u, v, inv, force, corner, *got, surface, *samples)


def ring(value, axis, steps):
    count = lax.axis_size(axis)
    return lax.ppermute(value, axis, [(s, (s + steps) % count) for s in range(count)])


def swap(value, axis, offset):
    count = lax.axis_size(axis)
    pairs = []
    for s in range(offset, count + offset, 2):
        pairs += [(s % count, (s + 1) % count), ((s + 1) % count, s % count)]
    return lax.ppermute(value, axis, pairs)


def body(gd, gv, gm, cd, cv, cm, lam, mu, dm, kept, den, hist, cells, filters):
    filters = filters.T
    state, message = load_nodes(gd, gv, cd, cv, den, hist, cells)
    rx = ring(message, "slab", -1)
    memory, sums, moduli = memory_part(gm, cm, lam, mu, dm)
    message = depth_message(state, rx, moduli)
    ry = ring(message, "depth", -1)
    part = filter_part(hist, cells, filters, rx, message)[None]
    u, v, inv, stress, strain, corner, first, second = first_step(
        state, rx, ry, moduli, sums
    )
    strains, samples = [strain], []
    for step in range(1, STEPS + 1):
        yb = swap(second, "depth", 1)
        ya = swap(first, "depth", 0)
        force = rest_of_forces(stress)
        corner, first, second, inner_first, inner_second = fold_depth(corner, force, ya, yb)
        xb = swap(second, "slab", 1)
        yb = swap(inner_second, "depth", 1)
        ya = swap(inner_first, "depth", 0)
        xa = swap(first, "slab", 0)
        got = (xa, xb, ya, yb)
        if step == 1:
            reach = 1
            while reach < lax.axis_size("depth"):
                part = join(part, ring(part, "depth", -reach), corner)
                reach *= 2
            surface = surface_part(part)
        if step < STEPS:
            sums = next_sums(step, kept, memory, strains)
            u, v, stress, strain, corner, first, second, sample = next_step(
                step, u, v, inv, force, corner, got, surface, moduli, sums, samples
            )
            strains.append(strain)
            samples.append(sample)
        else:
            gm_out, cm_out = final_memory(kept, memory, strains, gm.shape)
            gd_out, gv_out, cd_out, cv_out = finish(
                u, v, inv, force, corner, got, surface, samples, gd.shape
            )
    return gd_out, gv_out, gm_out, cd_out, cv_out, cm_out


def solution(mesh):
    nodes = P(None, "slab", "depth", None)
    memory = P(None, None, None, None, None, "slab", "depth", None)
    points = P(None, None, None, "slab", "depth", None)
    return jax.shard_map(
        body,
        mesh=mesh,
        in_specs=(
            nodes,
            nodes,
            memory,
            nodes,
            nodes,
            memory,
            points,
            points,
            points,
            P(),
            P("slab", "depth", None),
            P(None, "slab", "depth"),
            P("slab", "depth"),
            P(),
        ),
        out_specs=(nodes, nodes, memory, nodes, nodes, memory),
        check_vma=False,
    )
```
